32 devices in a mesh: groups: 2 (over y), brick: 16 (over z, x, core).
Axes of the slice: x: 2, y: 2, z: 4, core: 2. Of those that a mesh axis runs over, the one named last changes fastest.
Arguments:
- ct_win: bfloat16 [64, 128, 768], P(('groups', 'brick')), parts along dimension 0, may hold values from -8 to 8
- pet_win: bfloat16 [64, 128, 768], P(('groups', 'brick')), parts along dimension 0, may hold values from -8 to 8
- placed_anchor: int32 [64], P('groups'), parts along dimension 0, may hold values from 0 to 12, as said below
- placed_count: int32 [64], P('groups'), parts along dimension 0, may hold values from 0 to 256, as said below
- norm_ct: float32 [768], replicated, may hold values from 0.1 to 1.9
- norm_pet: float32 [768], replicated, may hold values from 0.1 to 1.9
- norm_ffn: float32 [768], replicated, may hold values from 0.1 to 1.9
- w_query: bfloat16 [768, 768], replicated, may hold values from -2 to 2
- w_key: bfloat16 [768, 768], replicated, may hold values from -2 to 2
- w_value: bfloat16 [768, 768], replicated, may hold values from -0.21875 to 0.21875
- w_out: bfloat16 [768, 768], replicated, may hold values from -0.21875 to 0.21875
- w_up: bfloat16 [768, 1536], replicated, may hold values from -0.21875 to 0.21875
- w_down: bfloat16 [1536, 768], replicated, may hold values from -0.15625 to 0.15625
- w_upconv: bfloat16 [768, 1024], replicated, may hold values from -0.21875 to 0.21875
- w_conv: bfloat16 [3456, 128], replicated, may hold values from -0.109375 to 0.109375
Outputs:
- volume: bfloat16 [64, 8, 16, 128], P(('groups', 'brick')), parts along dimension 0
The draws below stay inside these ranges and needn't reach their ends.
There are 2 independent parts, one for each index of `groups`. The reference program is written for one: setup_inputs(seed, part) draws one part's arguments, and reference() takes and returns one part's arrays. A program takes and returns all parts, laid end to end along the dimension named above; an argument that names none is the same for every part. Nothing has to cross between parts.
Inputs may be any that keep to these rules, and one draw needn't show every extreme that they name: `placed_anchor`: windows may lie anywhere in depth, whichever device holds them. `placed_count`: on each device the live slots (count above 0) are its first slots, at least one; in every draw some device has all 2 slots live and some device only one; a live window's count is 1 to 256, and 256 occurs in every draw.
All inputs are finite; a program needn't handle non-finite values.
Results may differ from the reference program's by a relative error of at most 0.012.
The reference program's roundings to bfloat16 on the way count: a program that leaves them out, or rounds other values in their place, can miss the bound.
Values may be sent and summed in bfloat16 or wider, within the bound.
A program may use at most 128 MiB of HBM per device.

```python
import jax
import jax.numpy as jnp
from jax import lax

D = 768
FF = 1536
DH = 64
HEADS = 12
CH = 128
PY = 4
PX = 8
WDEP = 4
CAP = 2
PLANE = 32
WT = 128
NZ = 16
NS = 32
N_BRICK = 16


def token_pair(key):
    base = jax.random.fold_in(key, 11)
    key_one, key_two = jax.random.split(base, 2)
    shape = (NS, WT, D)
    ct_vals = jax.random.normal(key_one, shape, jnp.float32)
    pet_vals = jax.random.normal(key_two, shape, jnp.float32)
    return (jnp.clip(ct_vals, -8.0, 8.0), jnp.clip(pet_vals, -8.0, 8.0))


def draw_ct_win(key, part):
    return token_pair(key)[0].astype(jnp.bfloat16)


def draw_pet_win(key, part):
    return token_pair(key)[1].astype(jnp.bfloat16)


def projection_pair(key):
    base = jax.random.fold_in(key, 23)
    key_one, key_two = jax.random.split(base, 2)
    scale_in = D ** (-0.5)
    own_query = jax.random.normal(key_one, (D, D), jnp.float32) * scale_in
    own_key = jax.random.normal(key_two, (D, D), jnp.float32) * scale_in
    query_mat = own_query
    key_mat = own_key
    return (jnp.clip(query_mat, -2.0, 2.0), jnp.clip(key_mat, -2.0, 2.0))


def draw_w_query(key, part):
    return projection_pair(key)[0].astype(jnp.bfloat16)


def draw_w_key(key, part):
    return projection_pair(key)[1].astype(jnp.bfloat16)


def draw_placed_anchor(key, part):
    base = jax.random.fold_in(key, 53)
    key_one, key_two = jax.random.split(base, 2)
    holder = jnp.arange(NS, dtype=jnp.int32) // CAP
    slot_ids = jnp.arange(NS, dtype=jnp.int32) % CAP
    far_plane = (holder + NZ // 2) % NZ
    back = jax.random.randint(key_one, (NS,), 0, WDEP)
    far_anchor = jnp.clip(far_plane - back, 0, NZ - WDEP)
    anywhere = jax.random.randint(key_two, (NS,), 0, NZ - WDEP + 1)
    return jnp.where(slot_ids == 0, far_anchor, anywhere).astype(jnp.int32)


def draw_placed_count(key, part):
    base = jax.random.fold_in(key, 37)
    key_one, key_two, key_three = jax.random.split(base, 3)
    live_slots = jax.random.randint(key_one, (NZ,), 1, CAP + 1)
    fullest = jax.random.randint(key_two, (), 0, NZ)
    live_slots = live_slots.at[fullest].set(CAP)
    live_slots = live_slots.at[(fullest + 1) % NZ].set(1)
    slot_ids = jnp.arange(CAP, dtype=jnp.int32)[None, :]
    live_mask = slot_ids < live_slots[:, None]
    counts = jax.random.randint(key_three, (NZ, CAP), 1, 2 * WT + 1)
    counts = counts.at[fullest, 0].set(2 * WT)
    return jnp.where(live_mask, counts, 0).reshape(NZ * CAP).astype(jnp.int32)


def normal_values(key, shape, deviation, limit, kind=jnp.bfloat16):
    values = deviation * jax.random.normal(key, shape, jnp.float32)
    return jnp.clip(values, min=-limit, max=limit).astype(kind)


def setup_inputs(seed: int = 0, part: int = 0) -> dict:
    splits = jax.random.split(jax.random.key(seed), 16)
    own_keys = jax.random.split(jax.random.fold_in(splits[15], part), 16)
    ct_win = draw_ct_win(jax.random.fold_in(jax.random.fold_in(splits[15], part), 71), part)
    pet_win = draw_pet_win(jax.random.fold_in(jax.random.fold_in(splits[15], part), 71), part)
    placed_anchor = draw_placed_anchor(jax.random.fold_in(jax.random.fold_in(splits[15], part), 71), part)
    placed_count = draw_placed_count(jax.random.fold_in(jax.random.fold_in(splits[15], part), 71), part)
    norm_ct = jnp.clip(1.0 + 0.18 * jax.random.normal(splits[4], (D,), jnp.float32), 0.1, 1.9)
    norm_pet = jnp.clip(1.0 + 0.18 * jax.random.normal(splits[5], (D,), jnp.float32), 0.1, 1.9)
    norm_ffn = jnp.clip(1.0 + 0.18 * jax.random.normal(splits[6], (D,), jnp.float32), 0.1, 1.9)
    w_query = draw_w_query(jax.random.fold_in(splits[15], 71), part)
    w_key = draw_w_key(jax.random.fold_in(splits[15], 71), part)
    w_value = normal_values(splits[9], (D, D), D ** -0.5, 0.21875)
    w_out = normal_values(splits[10], (D, D), D ** -0.5, 0.21875)
    w_up = normal_values(splits[11], (D, FF), D ** -0.5, 0.21875)
    w_down = normal_values(splits[12], (FF, D), FF ** -0.5, 0.15625)
    w_upconv = normal_values(splits[13], (D, 8 * CH), D ** -0.5, 0.21875)
    w_conv = normal_values(splits[14], (27 * CH, CH), (27 * CH) ** -0.5, 0.109375)
    return dict(ct_win=ct_win, pet_win=pet_win, placed_anchor=placed_anchor, placed_count=placed_count, norm_ct=norm_ct, norm_pet=norm_pet, norm_ffn=norm_ffn, w_query=w_query, w_key=w_key, w_value=w_value, w_out=w_out, w_up=w_up, w_down=w_down, w_upconv=w_upconv, w_conv=w_conv)


epsilon = 1e-06

def rms_scale(inputs, gain_vec):
    inputs = inputs.astype(jnp.float32)
    mean_square = lax.optimization_barrier(jnp.mean(inputs * inputs, axis=-1, keepdims=True))
    return (inputs * lax.rsqrt(mean_square + epsilon) * gain_vec).astype(jnp.bfloat16)

def project(normed, weight):
    return jnp.dot(normed, weight, preferred_element_type=jnp.float32).astype(jnp.bfloat16)

def attend(queries, key_rows, value_rows):
    row_total = queries.shape[0]
    query_heads = queries.astype(jnp.float32).reshape(row_total, HEADS, DH)
    key_heads = key_rows.astype(jnp.float32).reshape(row_total, HEADS, DH)
    value_heads = value_rows.astype(jnp.float32).reshape(row_total, HEADS, DH)
    scores = jnp.einsum('whd,vhd->hwv', query_heads, key_heads) / DH ** 0.5
    row_max = lax.optimization_barrier(jnp.max(scores, axis=-1, keepdims=True))
    exp_scores = jnp.exp(scores - row_max)
    attn_probs = (exp_scores / lax.optimization_barrier(jnp.sum(exp_scores, axis=-1, keepdims=True))).astype(jnp.bfloat16)
    mixed_out = jnp.einsum('hwv,vhd->whd', attn_probs.astype(jnp.float32), value_heads)
    return mixed_out.reshape(row_total, D).astype(jnp.bfloat16)

def feed_forward(middle, norm_ffn, w_up, w_down):
    normed = rms_scale(middle, norm_ffn)
    hidden = jax.nn.gelu(jnp.dot(normed, w_up, preferred_element_type=jnp.float32), approximate=True).astype(jnp.bfloat16)
    return middle + jnp.dot(hidden, w_down, preferred_element_type=jnp.float32)

def window_layer(ct_rows, pet_rows, params):
    norm_ct, norm_pet, norm_ffn, w_query, w_key, w_value, w_out, w_up, w_down = params
    normed_ct = rms_scale(ct_rows, norm_ct)
    normed_pet = rms_scale(pet_rows, norm_pet)
    mixed_ct = attend(project(normed_ct, w_query), project(normed_pet, w_key), project(normed_pet, w_value))
    mixed_pet = attend(project(normed_pet, w_query), project(normed_ct, w_key), project(normed_ct, w_value))
    mid_ct = ct_rows.astype(jnp.float32) + jnp.dot(mixed_ct, w_out, preferred_element_type=jnp.float32)
    mid_pet = pet_rows.astype(jnp.float32) + jnp.dot(mixed_pet, w_out, preferred_element_type=jnp.float32)
    return feed_forward(mid_ct, norm_ffn, w_up, w_down) + feed_forward(mid_pet, norm_ffn, w_up, w_down)

def reference(ct_win, pet_win, placed_anchor, placed_count, norm_ct, norm_pet, norm_ffn, w_query, w_key, w_value, w_out, w_up, w_down, w_upconv, w_conv):
    params = (norm_ct, norm_pet, norm_ffn, w_query, w_key, w_value, w_out, w_up, w_down)
    offsets = jnp.arange(WDEP, dtype=jnp.float32) - (WDEP - 1) / 2.0
    spread_width = WDEP / 4.0
    bell_curve = jnp.exp(-offsets * offsets / (2.0 * spread_width * spread_width))

    def holder_step(running, holder):
        start = holder * CAP
        ct_rows = lax.dynamic_slice_in_dim(ct_win, start, CAP)
        pet_rows = lax.dynamic_slice_in_dim(pet_win, start, CAP)
        count_rows = lax.dynamic_slice_in_dim(placed_count, start, CAP)
        anchor_rows = lax.dynamic_slice_in_dim(placed_anchor, start, CAP)

        def one_slot(slot_items):
            ct_one, pet_one, count_one = slot_items
            return lax.cond(count_one > 0, lambda: window_layer(ct_one, pet_one, params), lambda: jnp.zeros((WT, D), jnp.float32))
        joined = lax.map(one_slot, (ct_rows, pet_rows, count_rows))
        factor = count_rows.astype(jnp.float32) / (2.0 * WT)
        flat_terms = (joined.reshape(CAP, WDEP, PLANE * D) * (factor[:, None] * bell_curve[None, :])[:, :, None]).reshape(CAP * WDEP, PLANE * D)
        target = (anchor_rows[:, None] + jnp.arange(WDEP, dtype=jnp.int32)[None, :]).reshape(CAP * WDEP)
        one_hot = (jnp.arange(NZ, dtype=jnp.int32)[:, None] == target[None, :]).astype(jnp.float32)
        share = jnp.dot(one_hot, flat_terms, precision=lax.Precision.HIGHEST, preferred_element_type=jnp.float32).astype(jnp.bfloat16)
        return (running + lax.optimization_barrier(share).astype(jnp.float32), None)
    numerator, unused = lax.scan(holder_step, jnp.zeros((NZ, PLANE * D), jnp.float32), jnp.arange(N_BRICK, dtype=jnp.int32))
    planes = jnp.arange(NZ, dtype=jnp.int32)
    inside = (planes[:, None] >= placed_anchor[None, :]) & (planes[:, None] < placed_anchor[None, :] + WDEP)
    shifted = (planes[:, None] - placed_anchor[None, :]).astype(jnp.float32) - (WDEP - 1) / 2.0
    all_factor = placed_count.astype(jnp.float32) / (2.0 * WT)
    denominator = lax.optimization_barrier(jnp.sum(jnp.where(inside, all_factor[None, :] * jnp.exp(-shifted * shifted / (2.0 * spread_width * spread_width)), 0.0), axis=1))
    feature = (numerator / jnp.maximum(denominator, 1.0)[:, None]).astype(jnp.bfloat16)
    up_rows = jnp.dot(feature.reshape(NZ * PLANE, D), w_upconv, preferred_element_type=jnp.float32)
    up_rows = up_rows.reshape(NZ, PY, PX, 2, 2, 2, CH).transpose(0, 3, 1, 4, 2, 5, 6)
    upsampled = up_rows.reshape(2 * NZ, 2 * PY, 2 * PX, CH).astype(jnp.bfloat16)
    active = jnp.maximum(upsampled, 0).astype(jnp.float32)
    kernel = w_conv.astype(jnp.float32).reshape(3, 3, 3, CH, CH)
    conv_out = lax.conv_general_dilated(active[None], kernel, (1, 1, 1), 'SAME', dimension_numbers=('NDHWC', 'DHWIO', 'NDHWC'), precision=lax.Precision.HIGHEST)[0]
    return (upsampled.astype(jnp.float32) + conv_out).astype(jnp.bfloat16)
```

```python
import functools
import math

import jax
import jax.numpy as jnp
from jax import lax
from jax.experimental import pallas as pl
from jax.experimental.pallas import tpu as pltpu
from jax.sharding import PartitionSpec as P

DH = 64
PY = 4
PX = 8
WDEP = 4
SUB = 128

epsilon = 1e-06
F32 = jnp.float32
BF16 = jnp.bfloat16
MESH = pl.DeviceIdType.MESH


def rms_scale(inputs, gain_vec):
    mean_square = jnp.mean(inputs * inputs, axis=-1, keepdims=True)
    return (inputs * lax.rsqrt(mean_square + epsilon) * gain_vec).astype(BF16)


def matmul(left, right):
    return jnp.dot(left, right, preferred_element_type=F32)


def paired(index, step):
    value = 0
    bit = 1
    while bit <= step:
        digit = (index // bit) % 2
        value = value + bit * ((1 - digit) if (step // bit) % 2 else digit)
        bit *= 2
    return value + (index // bit) * bit


def bell_at(depth):
    spread = WDEP / 4.0
    value = jnp.float32(0.0)
    for i in range(WDEP):
        offset = i - (WDEP - 1) / 2.0
        value = jnp.where(depth == i, jnp.float32(math.exp(-offset * offset / (2.0 * spread * spread))), value)
    return value


def kernel(
    bricks,
    anchor_ref, count_ref, gain_ct, gain_pet, gain_ffn,
    ct_hbm, pet_hbm, wq_hbm, wk_hbm, wv_hbm, wo_hbm, wup_hbm, wdown_hbm, wupc_hbm, wconv_hbm,
    out_ref,
    tokens, wq, wk, wv, wo, wup, wdown, wupc, wconv,
    normed, queries, keys, values, mixed, middle, hidden, joined,
    share, got_core, sum_x, got_x, sum_z, got_z,
    fine, halo_fine, edge, got_edge, patches,
    load_sem, send_core, recv_core, send_x, recv_x, send_z, recv_z, send_edge, recv_edge,
):
    position = lax.axis_index("brick")
    ring = bricks // 4
    core = position % 2
    side = (position // 2) % 2
    deep = position // 4
    partner_core = position + 1 - 2 * core
    partner_side = position + 2 - 4 * side

    barrier = pltpu.get_barrier_semaphore()

    def greet(target):
        pl.semaphore_signal(barrier, inc=1, device_id={"brick": target}, device_id_type=MESH)

    greet(partner_core)
    greet(partner_side)
    for step in range(1, ring):
        greet(paired(deep, step) * 4 + position % 4)

    inside = (position > 0) & (position < bricks - 1)

    @pl.when(inside)
    def _():
        greet(position - 1 + 2 * core)

    slots, window_tokens, width = ct_hbm.shape
    rows = slots * window_tokens
    loads = [
        pltpu.make_async_copy(src, dst, load_sem.at[i])
        for i, (src, dst) in enumerate(
            (
                (ct_hbm, tokens.at[0]), (pet_hbm, tokens.at[1]),
                (wq_hbm, wq), (wk_hbm, wk), (wv_hbm, wv), (wo_hbm, wo),
                (wup_hbm, wup), (wdown_hbm, wdown), (wupc_hbm, wupc), (wconv_hbm, wconv),
            )
        )
    ]
    for i in range(5):
        loads[i].start()

    fine[...] = jnp.zeros_like(fine)
    halo_fine[...] = jnp.zeros_like(halo_fine)
    patches[...] = jnp.zeros_like(patches)

    for m, gain in enumerate((gain_ct, gain_pet)):
        loads[m].wait()
        for s in range(slots):
            normed[pl.ds(m * rows + s * window_tokens, window_tokens), :] = rms_scale(
                tokens[m, s].astype(F32), gain[...].reshape(1, width)
            )
    for i in range(5, 10):
        loads[i].start()
    for i, (weight, result) in enumerate(((wq, queries), (wk, keys), (wv, values))):
        loads[2 + i].wait()
        result[...] = matmul(normed[...], weight[...]).astype(BF16)

    lane = lax.broadcasted_iota(jnp.int32, (1, SUB), 1)
    low_half = (lane < DH)
    low = jnp.where(low_half, 1.0, 0.0).astype(BF16)
    high = jnp.where(low_half, 0.0, 1.0).astype(BF16)
    for m in range(2):
        for s in range(slots):
            own = pl.ds(m * rows + s * window_tokens, window_tokens)
            other = pl.ds((1 - m) * rows + s * window_tokens, window_tokens)
            for pair in range(width // SUB):
                cols = pl.ds(pair * SUB, SUB)
                query = queries[own, cols]
                query = jnp.concatenate([query * low, query * high], axis=0)
                scores = lax.dot_general(
                    query, keys[other, cols], (((1,), (1,)), ((), ())), preferred_element_type=F32
                )
                row_max = jnp.max(scores, axis=-1, keepdims=True)
                exp_scores = jnp.exp((scores - row_max) * (1.0 / DH**0.5))
                inverse = 1.0 / jnp.sum(exp_scores, axis=-1, keepdims=True)
                probs = (exp_scores * inverse).astype(BF16)
                heads = matmul(probs, values[other, cols])
                mixed[own, cols] = jnp.where(
                    low_half, heads[:window_tokens], heads[window_tokens:]
                ).astype(BF16)

    loads[5].wait()
    for m in range(2):
        half = pl.ds(m * rows, rows)
        mid = tokens[m].reshape(rows, width).astype(F32) + matmul(mixed[half, :], wo[...])
        middle[half, :] = mid
        normed[half, :] = rms_scale(mid, gain_ffn[...].reshape(1, width))
    loads[6].wait()
    inner = wup.shape[1]
    block = 512 if inner % 512 == 0 else inner
    for start in range(0, inner, block):
        cols = pl.ds(start, block)
        first = jax.nn.gelu(matmul(normed[pl.ds(0, rows), :], wup[:, cols]), approximate=True)
        second = jax.nn.gelu(matmul(normed[pl.ds(rows, rows), :], wup[:, cols]), approximate=True)
        hidden[:, cols] = (first + second).astype(BF16)
    loads[7].wait()
    total = middle[pl.ds(0, rows), :] + middle[pl.ds(rows, rows), :] + matmul(hidden[...], wdown[...])
    joined[...] = total.reshape(joined.shape)

    anchors = [anchor_ref[position * slots + s] for s in range(slots)]
    factors = [
        count_ref[position * slots + s].astype(F32) * (1.0 / (2.0 * window_tokens)) for s in range(slots)
    ]

    def blend(at_core, at_side):
        for z in range(ring):
            plane = z * 4 + at_side * 2 + at_core
            term = None
            for s in range(slots):
                depth = plane - anchors[s]
                weight = factors[s] * bell_at(depth)
                piece = joined[s * WDEP + jnp.clip(depth, 0, WDEP - 1)] * weight
                term = piece if term is None else term + piece
            share[at_core, at_side, z] = term.astype(BF16)

    blend(1 - core, 1 - side)

    pl.semaphore_wait(barrier, jnp.where(inside, ring + 2, ring + 1))

    def remote(src, dst, send, recv, target):
        return pltpu.make_async_remote_copy(
            src_ref=src, dst_ref=dst, send_sem=send, recv_sem=recv,
            device_id={"brick": target}, device_id_type=MESH,
        )

    def core_copy(sent):
        return remote(
            share.at[1 - core, sent], got_core.at[sent],
            send_core.at[sent], recv_core.at[sent], partner_core,
        )

    core_copy(1 - side).start()
    blend(1 - core, side)
    core_copy(side).start()
    blend(core, 1 - side)
    blend(core, side)
    order = list(range(ring - 1, 0, -1)) + [0]

    def side_copy(z):
        return remote(sum_x.at[z], got_x.at[z], send_x.at[z], recv_x.at[z], partner_side)

    core_copy(1 - side).wait()
    for step in order:
        z = paired(deep, step)
        sum_x[z] = (share[core, 1 - side, z].astype(F32) + got_core[1 - side, z].astype(F32)).astype(BF16)
        side_copy(z).start()
    core_copy(side).wait()

    def deep_copy(step):
        z = paired(deep, step)
        return remote(
            sum_z.at[z], got_z.at[deep], send_z.at[z], recv_z.at[deep], z * 4 + position % 4
        )

    def arrival(step):
        z = paired(deep, step)
        return z, remote(
            sum_z.at[z], got_z.at[z], send_z.at[z], recv_z.at[z], z * 4 + position % 4
        )

    numerator = None
    for step in order:
        z = paired(deep, step)
        side_copy(z).wait_recv()
        partial = (
            share[core, side, z].astype(F32) + got_core[side, z].astype(F32) + got_x[z].astype(F32)
        )
        if step:
            sum_z[z] = partial.astype(BF16)
            deep_copy(step).start()
        else:
            numerator = partial

    def weigh(s, value):
        return value + bell_at(position - anchor_ref[s]) * (
            count_ref[s].astype(F32) * (1.0 / (2.0 * window_tokens))
        )

    denominator = lax.fori_loop(0, bricks * slots, weigh, jnp.float32(0.0))
    loads[8].wait()
    loads[9].wait()
    for step in range(1, ring):
        z, landed = arrival(step)
        landed.wait_recv()
        numerator = numerator + got_z[z].astype(F32)
    for step in order:
        side_copy(paired(deep, step)).wait_send()
        if step:
            deep_copy(step).wait_send()

    feature = (numerator / jnp.maximum(denominator, 1.0)).astype(BF16)
    channels = wconv.shape[1]
    raised = matmul(feature, wupc[...]).astype(BF16).astype(F32)
    for a in range(2):
        for b in range(2):
            for c in range(2):
                at = ((a * 2 + b) * 2 + c) * channels
                for y in range(PY):
                    fine[a, 2 * y + b, pl.ds(8 + c, PX, stride=2), :] = raised[
                        y * PX : (y + 1) * PX, at : at + channels
                    ]
    for a in range(2):
        edge[a] = jnp.maximum(fine[a, :, 8 : 8 + 2 * PX, :], 0.0).astype(BF16)

    def edge_left():
        return remote(edge.at[0], got_edge.at[1], send_edge.at[0], recv_edge.at[1], position - 1)

    def edge_right():
        return remote(edge.at[1], got_edge.at[0], send_edge.at[1], recv_edge.at[0], position + 1)

    @pl.when(position > 0)
    def _():
        edge_left().start()

    @pl.when(position < bricks - 1)
    def _():
        edge_right().start()

    line = 2 * PX
    plane_rows = 2 * PY * line

    def fill(source, a, layer):
        for y in range(2 * PY):
            for dx in range(3):
                patches[layer, pl.ds((1 + y) * line, line), pl.ds(dx * channels, channels)] = jnp.maximum(
                    source[a, y, 7 + dx : 7 + dx + line, :], 0.0
                ).astype(BF16)

    def taps(layer, dz):
        acc = None
        for dy in range(3):
            term = matmul(
                patches[layer, pl.ds(dy * line, plane_rows), :],
                wconv[pl.ds((dz * 3 + dy) * 3 * channels, 3 * channels), :],
            )
            acc = term if acc is None else acc + term
        return acc

    fill(fine, 0, 1)
    fill(fine, 1, 2)
    upper = taps(1, 1) + taps(2, 2)
    lower = taps(1, 0) + taps(2, 1)

    @pl.when(position > 0)
    def _():
        edge_left().wait_send()
        remote(edge.at[1], got_edge.at[0], send_edge.at[1], recv_edge.at[0], position - 1).wait_recv()
        halo_fine[0, :, 8 : 8 + line, :] = got_edge[0].astype(F32)

    @pl.when(position < bricks - 1)
    def _():
        edge_right().wait_send()
        remote(edge.at[0], got_edge.at[1], send_edge.at[0], recv_edge.at[1], position + 1).wait_recv()
        halo_fine[1, :, 8 : 8 + line, :] = got_edge[1].astype(F32)

    fill(halo_fine, 0, 0)
    fill(halo_fine, 1, 3)
    upper = upper + taps(0, 0)
    lower = lower + taps(3, 2)
    for a, conv in enumerate((upper, lower)):
        own = fine[a, :, 8 : 8 + line, :]
        out_ref[a] = (own + conv.reshape(own.shape)).astype(BF16)


def on_device(
    ct_win, pet_win, placed_anchor, placed_count, norm_ct, norm_pet, norm_ffn,
    w_query, w_key, w_value, w_out, w_up, w_down, w_upconv, w_conv,
):
    slots, window_tokens, width = ct_win.shape
    rows = slots * window_tokens
    bricks = lax.axis_size("brick")
    ring = bricks // 4
    cells = window_tokens // WDEP
    channels = w_conv.shape[1]
    line = 2 * PX
    dma = pltpu.SemaphoreType.DMA
    plane = (cells, width)

    def like(array):
        return pltpu.VMEM(array.shape, array.dtype)

    smem = pl.BlockSpec(memory_space=pltpu.SMEM)
    vmem = pl.BlockSpec(memory_space=pltpu.VMEM)
    hbm = pl.BlockSpec(memory_space=pl.ANY)
    return pl.pallas_call(
        functools.partial(kernel, bricks),
        out_shape=pltpu.VMEM((2, 2 * PY, line, channels), BF16),
        in_specs=[smem] * 2 + [vmem] * 3 + [hbm] * 10,
        out_specs=vmem,
        scratch_shapes=[
            pltpu.VMEM((2,) + ct_win.shape, BF16),
            like(w_query), like(w_key), like(w_value), like(w_out), like(w_up), like(w_down),
            like(w_upconv), like(w_conv),
            pltpu.VMEM((2 * rows, width), BF16),
            pltpu.VMEM((2 * rows, width), BF16),
            pltpu.VMEM((2 * rows, width), BF16),
            pltpu.VMEM((2 * rows, width), BF16),
            pltpu.VMEM((2 * rows, width), BF16),
            pltpu.VMEM((2 * rows, width), F32),
            pltpu.VMEM((rows, w_up.shape[1]), BF16),
            pltpu.VMEM((slots * WDEP,) + plane, F32),
            pltpu.VMEM((2, 2, ring) + plane, BF16),
            pltpu.VMEM((2, ring) + plane, BF16),
            pltpu.VMEM((ring,) + plane, BF16),
            pltpu.VMEM((ring,) + plane, BF16),
            pltpu.VMEM((ring,) + plane, BF16),
            pltpu.VMEM((ring,) + plane, BF16),
            pltpu.VMEM((2, 2 * PY, line + 16, channels), F32),
            pltpu.VMEM((2, 2 * PY, line + 16, channels), F32),
            pltpu.VMEM((2, 2 * PY, line, channels), BF16),
            pltpu.VMEM((2, 2 * PY, line, channels), BF16),
            pltpu.VMEM((4, (2 * PY + 2) * line, 3 * channels), BF16),
            dma((10,)), dma((2,)), dma((2,)), dma((ring,)), dma((ring,)),
            dma((ring,)), dma((ring,)), dma((2,)), dma((2,)),
        ],
        compiler_params=pltpu.CompilerParams(collective_id=0, has_side_effects=True),
        name="windows",
    )(
        placed_anchor, placed_count, norm_ct, norm_pet, norm_ffn,
        ct_win, pet_win, w_query, w_key, w_value, w_out, w_up, w_down, w_upconv, w_conv,
    )


def solution(mesh):
    split = P(("groups", "brick"), None, None)
    return jax.shard_map(
        on_device,
        mesh=mesh,
        in_specs=(split, split, P("groups"), P("groups")) + (P(),) * 11,
        out_specs=P(("groups", "brick"), None, None, None),
        check_vma=False,
    )
```

```python
import functools
import math

import jax
import jax.numpy as jnp
from jax import lax
from jax.experimental import pallas as pl
from jax.experimental.pallas import tpu as pltpu
from jax.sharding import PartitionSpec as P

DH = 64
PY = 4
PX = 8
WDEP = 4
SUB = 128

epsilon = 1e-06
F32 = jnp.float32
BF16 = jnp.bfloat16
MESH = pl.DeviceIdType.MESH


def rms_scale(inputs, gain_vec):
    mean_square = jnp.mean(inputs * inputs, axis=-1, keepdims=True)
    return (inputs * lax.rsqrt(mean_square + epsilon) * gain_vec).astype(BF16)


def matmul(left, right):
    return jnp.dot(left, right, preferred_element_type=F32)


def paired(index, step):
    value = 0
    bit = 1
    while bit <= step:
        digit = (index // bit) % 2
        value = value + bit * ((1 - digit) if (step // bit) % 2 else digit)
        bit *= 2
    return value + (index // bit) * bit


def bell_at(depth):
    spread = WDEP / 4.0
    value = jnp.where(depth == depth, jnp.float32(0.0), jnp.float32(0.0))
    for i in range(WDEP):
        offset = i - (WDEP - 1) / 2.0
        value = jnp.where(depth == i, jnp.float32(math.exp(-offset * offset / (2.0 * spread * spread))), value)
    return value


def kernel(
    bricks,
    anchor_hbm, count_hbm, gain_ct_hbm, gain_pet_hbm, gain_ffn_hbm,
    ct_hbm, pet_hbm, wq_hbm, wk_hbm, wv_hbm, wo_hbm, wup_hbm, wdown_hbm, wupc_hbm, wconv_hbm,
    out_ref,
    anchor_ref, count_ref, anchor_row, count_row, gain_ct, gain_pet, gain_ffn,
    tokens, wq, wk, wv, wo, wup, wdown, wupc, wconv,
    normed, queries, keys, values, mixed, middle, hidden, joined,
    share, got, early, sum_z, got_z,
    fine, halo_fine, edge, got_edge, patches,
    load_sem, send_x, recv_x, send_z, recv_z, send_edge, recv_edge,
):
    position = lax.axis_index("brick")
    ring = bricks // 4
    place = position % 4
    core = position % 2
    deep = position // 4

    slots, window_tokens, width = ct_hbm.shape
    rows = 2 * window_tokens
    cells = window_tokens // WDEP
    channels = wconv.shape[1]
    inner = wup.shape[1]
    pieces, cut = sum_z.shape[0], sum_z.shape[3]

    plan = {
        "ct": (ct_hbm, tokens.at[0]), "pet": (pet_hbm, tokens.at[1]),
        "gain_ct": (gain_ct_hbm, gain_ct), "gain_pet": (gain_pet_hbm, gain_pet),
        "wq": (wq_hbm, wq), "wk": (wk_hbm, wk), "wv": (wv_hbm, wv),
        "gain_ffn": (gain_ffn_hbm, gain_ffn),
        "wo": (wo_hbm, wo), "wup": (wup_hbm, wup), "wdown": (wdown_hbm, wdown),
        "anchor": (anchor_hbm, anchor_ref), "count": (count_hbm, count_ref),
        "anchor_row": (anchor_hbm, anchor_row), "count_row": (count_hbm, count_row),
        "wupc": (wupc_hbm, wupc), "wconv": (wconv_hbm, wconv),
    }
    loads = {
        name: pltpu.make_async_copy(src, dst, load_sem.at[i]) for i, (name, (src, dst)) in enumerate(plan.items())
    }
    names = list(plan)
    waited = set()

    def load(*which):
        for name in which:
            loads[name].start()

    def ready(*which):
        for name in which:
            if name not in waited:
                waited.add(name)
                loads[name].wait()

    load(*names[:7])

    barrier = pltpu.get_barrier_semaphore()

    def greet(target):
        pl.semaphore_signal(barrier, inc=1, device_id={"brick": target}, device_id_type=MESH)

    def near(turn):
        return position + sum(
            bit * (1 - 2 * ((position // bit) % 2)) for bit in (1, 2) if (turn // bit) % 2
        )

    for turn in range(1, 4):
        greet(near(turn))
    for step in range(1, ring):
        greet(paired(deep, step) * 4 + place)
    bridge = ((place == 0) & (deep > 0)) | ((place == 3) & (deep < ring - 1))

    @pl.when(bridge)
    def _():
        greet(position - 1 + 2 * core)

    load(*names[7:])
    entered = []

    def enter():
        if not entered:
            entered.append(1)
            pl.semaphore_wait(barrier, jnp.where(bridge, ring + 3, ring + 2))

    fine[...] = jnp.zeros_like(fine)
    halo_fine[...] = jnp.zeros_like(halo_fine)
    patches[...] = jnp.zeros_like(patches)

    def token_rows(s, m):
        return pl.ds(s * rows + m * window_tokens, window_tokens)

    def project(s):
        both = pl.ds(s * rows, rows)
        for m, gain in enumerate((gain_ct, gain_pet)):
            ready(("ct", "pet")[m], ("gain_ct", "gain_pet")[m])
            normed[token_rows(s, m), :] = rms_scale(tokens[m, s].astype(F32), gain[...].reshape(1, width))
        for name, weight, result in (("wq", wq, queries), ("wk", wk, keys), ("wv", wv, values)):
            ready(name)
            result[both, :] = matmul(normed[both, :], weight[...]).astype(BF16)

    low_half = lax.broadcasted_iota(jnp.int32, (1, SUB), 1) < DH
    low = jnp.where(low_half, 1.0, 0.0).astype(BF16)
    high = jnp.where(low_half, 0.0, 1.0).astype(BF16)
    ones = jnp.concatenate(
        [jnp.broadcast_to(low, (window_tokens, SUB)), jnp.broadcast_to(high, (window_tokens, SUB))], axis=0
    )

    def attention(s):
        for m in range(2):
            own, other = token_rows(s, m), token_rows(s, 1 - m)
            for pair in range(width // SUB):
                cols = pl.ds(pair * SUB, SUB)
                key = keys[other, cols]
                value = values[other, cols]
                scores = lax.dot_general(
                    queries[own, cols], jnp.concatenate([key * low, key * high], axis=0),
                    (((1,), (1,)), ((), ())), preferred_element_type=F32,
                )
                probs = []
                for h in range(2):
                    part = scores[:, h * window_tokens : (h + 1) * window_tokens]
                    row_max = jnp.max(part, axis=-1, keepdims=True)
                    probs.append(jnp.exp2((part - row_max) * (math.log2(math.e) / DH**0.5)).astype(BF16))
                heads = matmul(
                    jnp.concatenate(probs, axis=1),
                    jnp.concatenate([jnp.concatenate([value * low, value * high], axis=0), ones], axis=1),
                )
                mixed[own, cols] = (heads[:, :SUB] / heads[:, SUB:]).astype(BF16)

    def forward(s):
        both = pl.ds(s * rows, rows)
        ready("wo", "gain_ffn")
        for m in range(2):
            own = token_rows(s, m)
            mid = tokens[m, s].astype(F32) + matmul(mixed[own, :], wo[...])
            middle[own, :] = mid
            normed[own, :] = rms_scale(mid, gain_ffn[...].reshape(1, width))
        ready("wup")
        block = 512 if inner % 512 == 0 else inner
        for start in range(0, inner, block):
            cols = pl.ds(start, block)
            active = jax.nn.gelu(matmul(normed[both, :], wup[:, cols]), approximate=True)
            hidden[pl.ds(s * window_tokens, window_tokens), cols] = (
                active[:window_tokens] + active[window_tokens:]
            ).astype(BF16)

    def lower(s, c):
        ready("wdown")
        cols = pl.ds(c * cut, cut)
        total = (
            middle[token_rows(s, 0), cols] + middle[token_rows(s, 1), cols]
            + matmul(hidden[pl.ds(s * window_tokens, window_tokens), :], wdown[:, cols])
        )
        joined[s, c] = total.astype(BF16).reshape(WDEP, cells, cut)

    def remote(src, dst, send, recv, target):
        return pltpu.make_async_remote_copy(
            src_ref=src, dst_ref=dst, send_sem=send, recv_sem=recv,
            device_id={"brick": target}, device_id_type=MESH,
        )

    def near_copy(s, c, turn):
        return remote(
            share.at[s, c, turn], got.at[s, c, turn], send_x.at[s, c, turn], recv_x.at[s, c, turn], near(turn)
        )

    def depth_of(anchor, at):
        return jnp.bitwise_and(at - anchor, WDEP - 1)

    def send_near(s, c):
        anchor = anchor_ref[position * slots + s]
        for turn in (3, 2, 1, 0):
            share[s, c, turn] = joined[s, c, depth_of(anchor, near(turn) % 4)]
            if turn:
                near_copy(s, c, turn).start()

    def landed(s, turn, z):
        slot = near(turn) * slots + s
        anchor = anchor_ref[slot]
        depth = depth_of(anchor, place)
        weight = count_ref[slot].astype(F32) * (1.0 / (2.0 * window_tokens)) * bell_at(depth)
        return jnp.where((anchor + depth) // 4 == z, weight, 0.0)

    def gather(s, c, z):
        total = None
        for turn in range(4):
            block = (got if turn else share)[s, c, turn].astype(F32) * landed(s, turn, z)
            total = block if total is None else total + block
        return total

    order = list(range(ring - 1, 0, -1)) + [0]

    def deep_copy(c, step):
        z = paired(deep, step)
        return remote(
            sum_z.at[c, z], got_z.at[c, deep], send_z.at[c, z], recv_z.at[c, deep], z * 4 + place
        )

    def arrival(c, step):
        z = paired(deep, step)
        return z, remote(
            sum_z.at[c, z], got_z.at[c, z], send_z.at[c, z], recv_z.at[c, z], z * 4 + place
        )

    last = slots - 1
    for s in range(slots):
        project(s)
        attention(s)
        forward(s)
        if s == 0:
            ready("anchor", "count")
            enter()
        for c in range(pieces):
            lower(s, c)
            send_near(s, c)
    for s in range(last):
        for c in range(pieces):
            for turn in range(1, 4):
                near_copy(s, c, turn).wait_recv()
            for step in order:
                z = paired(deep, step)
                block = gather(s, c, z)
                early[c, z] = block if s == 0 else early[c, z] + block

    own_sum = []
    for c in range(pieces):
        for turn in range(1, 4):
            near_copy(last, c, turn).wait_recv()
        for step in order:
            z = paired(deep, step)
            total = gather(last, c, z)
            if last:
                total = total + early[c, z]
            if step:
                sum_z[c, z] = total.astype(BF16)
                deep_copy(c, step).start()
            else:
                own_sum.append(total)

    ready("anchor_row", "count_row", "wupc", "wconv")
    row = (1, bricks * slots)
    denominator = jnp.sum(
        bell_at(position - anchor_row[...].reshape(row))
        * (count_row[...].reshape(row).astype(F32) * (1.0 / (2.0 * window_tokens))),
        axis=-1, keepdims=True,
    )
    inverse = 1.0 / jnp.maximum(denominator, 1.0)
    raised = None
    for c in range(pieces):
        numerator = own_sum[c]
        for step in range(1, ring):
            z, copy = arrival(c, step)
            copy.wait_recv()
            numerator = numerator + got_z[c, z].astype(F32)
        feature = (numerator * inverse).astype(BF16)
        part = matmul(feature, wupc[pl.ds(c * cut, cut), :])
        raised = part if raised is None else raised + part
    raised = raised.astype(BF16).astype(F32)
    for a in range(2):
        for b in range(2):
            for c in range(2):
                at = ((a * 2 + b) * 2 + c) * channels
                for y in range(PY):
                    fine[a, 2 * y + b, pl.ds(8 + c, PX, stride=2), :] = raised[
                        y * PX : (y + 1) * PX, at : at + channels
                    ]
    for a in range(2):
        edge[a] = jnp.maximum(fine[a, :, 8 : 8 + 2 * PX, :], 0.0).astype(BF16)

    def edge_left():
        return remote(edge.at[0], got_edge.at[1], send_edge.at[0], recv_edge.at[1], position - 1)

    def edge_right():
        return remote(edge.at[1], got_edge.at[0], send_edge.at[1], recv_edge.at[0], position + 1)

    @pl.when(position > 0)
    def _():
        edge_left().start()

    @pl.when(position < bricks - 1)
    def _():
        edge_right().start()

    line = 2 * PX
    plane_rows = 2 * PY * line

    def fill(source, a, layer):
        for y in range(2 * PY):
            for dx in range(3):
                patches[layer, pl.ds((1 + y) * line, line), pl.ds(dx * channels, channels)] = jnp.maximum(
                    source[a, y, 7 + dx : 7 + dx + line, :], 0.0
                ).astype(BF16)

    def taps(layer, dz):
        acc = None
        for dy in range(3):
            term = matmul(
                patches[layer, pl.ds(dy * line, plane_rows), :],
                wconv[pl.ds((dz * 3 + dy) * 3 * channels, 3 * channels), :],
            )
            acc = term if acc is None else acc + term
        return acc

    fill(fine, 0, 1)
    fill(fine, 1, 2)
    upper = taps(1, 1) + taps(2, 2)
    lower_ = taps(1, 0) + taps(2, 1)

    for c in range(pieces):
        for s in range(slots):
            for turn in range(1, 4):
                near_copy(s, c, turn).wait_send()
        for step in range(1, ring):
            deep_copy(c, step).wait_send()

    @pl.when(position > 0)
    def _():
        edge_left().wait_send()
        remote(edge.at[1], got_edge.at[0], send_edge.at[1], recv_edge.at[0], position - 1).wait_recv()
        halo_fine[0, :, 8 : 8 + line, :] = got_edge[0].astype(F32)

    @pl.when(position < bricks - 1)
    def _():
        edge_right().wait_send()
        remote(edge.at[0], got_edge.at[1], send_edge.at[0], recv_edge.at[1], position + 1).wait_recv()
        halo_fine[1, :, 8 : 8 + line, :] = got_edge[1].astype(F32)

    fill(halo_fine, 0, 0)
    fill(halo_fine, 1, 3)
    upper = upper + taps(0, 0)
    lower_ = lower_ + taps(3, 2)
    for a, conv in enumerate((upper, lower_)):
        own = fine[a, :, 8 : 8 + line, :]
        out_ref[a] = (own + conv.reshape(own.shape)).astype(BF16)


def on_device(
    ct_win, pet_win, placed_anchor, placed_count, norm_ct, norm_pet, norm_ffn,
    w_query, w_key, w_value, w_out, w_up, w_down, w_upconv, w_conv,
):
    slots, window_tokens, width = ct_win.shape
    rows = 2 * slots * window_tokens
    bricks = lax.axis_size("brick")
    ring = bricks // 4
    cells = window_tokens // WDEP
    channels = w_conv.shape[1]
    line = 2 * PX
    cut = 256 if width % 256 == 0 else width
    pieces = width // cut
    dma = pltpu.SemaphoreType.DMA
    block = (cells, cut)

    def like(array):
        return pltpu.VMEM(array.shape, array.dtype)

    return pl.pallas_call(
        functools.partial(kernel, bricks),
        out_shape=pltpu.VMEM((2, 2 * PY, line, channels), BF16),
        in_specs=[pl.BlockSpec(memory_space=pl.ANY)] * 15,
        out_specs=pl.BlockSpec(memory_space=pltpu.VMEM),
        scratch_shapes=[
            pltpu.SMEM(placed_anchor.shape, jnp.int32), pltpu.SMEM(placed_count.shape, jnp.int32),
            like(placed_anchor), like(placed_count), like(norm_ct), like(norm_pet), like(norm_ffn),
            pltpu.VMEM((2,) + ct_win.shape, BF16),
            like(w_query), like(w_key), like(w_value), like(w_out), like(w_up), like(w_down),
            like(w_upconv), like(w_conv),
            pltpu.VMEM((rows, width), BF16),
            pltpu.VMEM((rows, width), BF16),
            pltpu.VMEM((rows, width), BF16),
            pltpu.VMEM((rows, width), BF16),
            pltpu.VMEM((rows, width), BF16),
            pltpu.VMEM((rows, width), F32),
            pltpu.VMEM((slots * window_tokens, w_up.shape[1]), BF16),
            pltpu.VMEM((slots, pieces, WDEP) + block, BF16),
            pltpu.VMEM((slots, pieces, 4) + block, BF16),
            pltpu.VMEM((slots, pieces, 4) + block, BF16),
            pltpu.VMEM((pieces, ring) + block, F32),
            pltpu.VMEM((pieces, ring) + block, BF16),
            pltpu.VMEM((pieces, ring) + block, BF16),
            pltpu.VMEM((2, 2 * PY, line + 16, channels), F32),
            pltpu.VMEM((2, 2 * PY, line + 16, channels), F32),
            pltpu.VMEM((2, 2 * PY, line, channels), BF16),
            pltpu.VMEM((2, 2 * PY, line, channels), BF16),
            pltpu.VMEM((4, (2 * PY + 2) * line, 3 * channels), BF16),
            dma((17,)), dma((slots, pieces, 4)), dma((slots, pieces, 4)),
            dma((pieces, ring)), dma((pieces, ring)), dma((2,)), dma((2,)),
        ],
        compiler_params=pltpu.CompilerParams(
            collective_id=0, has_side_effects=True, vmem_limit_bytes=62 * 1024 * 1024
        ),
        name="windows",
    )(
        placed_anchor, placed_count, norm_ct, norm_pet, norm_ffn,
        ct_win, pet_win, w_query, w_key, w_value, w_out, w_up, w_down, w_upconv, w_conv,
    )


def solution(mesh):
    split = P(("groups", "brick"), None, None)
    return jax.shard_map(
        on_device,
        mesh=mesh,
        in_specs=(split, split, P("groups"), P("groups")) + (P(),) * 11,
        out_specs=P(("groups", "brick"), None, None, None),
        check_vma=False,
    )
```

```python
import functools
import math

import jax
import jax.numpy as jnp
from jax import lax
from jax.experimental import pallas as pl
from jax.experimental.pallas import tpu as pltpu
from jax.sharding import PartitionSpec as P

DH = 64
PY = 4
PX = 8
WDEP = 4
SUB = 128

epsilon = 1e-06
F32 = jnp.float32
BF16 = jnp.bfloat16
MESH = pl.DeviceIdType.MESH


def rms_scale(inputs, gain_vec):
    mean_square = jnp.mean(inputs * inputs, axis=-1, keepdims=True)
    return (inputs * lax.rsqrt(mean_square + epsilon) * gain_vec).astype(BF16)


def matmul(left, right):
    return jnp.dot(left, right, preferred_element_type=F32)


def paired(index, step):
    value = 0
    bit = 1
    while bit <= step:
        digit = (index // bit) % 2
        value = value + bit * ((1 - digit) if (step // bit) % 2 else digit)
        bit *= 2
    return value + (index // bit) * bit


def bell_at(depth):
    spread = WDEP / 4.0
    value = jnp.where(depth == depth, jnp.float32(0.0), jnp.float32(0.0))
    for i in range(WDEP):
        offset = i - (WDEP - 1) / 2.0
        value = jnp.where(depth == i, jnp.float32(math.exp(-offset * offset / (2.0 * spread * spread))), value)
    return value


def kernel(
    bricks,
    anchor_hbm, count_hbm, gain_ct_hbm, gain_pet_hbm, gain_ffn_hbm,
    ct_hbm, pet_hbm, wq_hbm, wk_hbm, wv_hbm, wo_hbm, wup_hbm, wdown_hbm, wupc_hbm, wconv_hbm,
    out_ref,
    anchor_ref, count_ref, anchor_row, count_row, gain_ct, gain_pet, gain_ffn,
    tokens, wq, wk, wv, wo, wup, wdown, wupc, wconv,
    normed, queries, keys, values, mixed, middle, hidden, joined,
    share, got, early, sum_z, got_z,
    fine, halo_fine, edge, got_edge, patches,
    load_sem, send_x, recv_x, send_z, recv_z, send_edge, recv_edge,
):
    position = lax.axis_index("brick")
    ring = bricks // 4
    place = position % 4
    core = position % 2
    side = (position // 2) % 2
    kept = place + 1 - 2 * core
    deep = position // 4

    slots, window_tokens, width = ct_hbm.shape
    rows = 2 * window_tokens
    cells = window_tokens // WDEP
    channels = wconv.shape[1]
    inner = wup.shape[1]
    pieces, cut = sum_z.shape[0], sum_z.shape[3]

    plan = {
        "ct": (ct_hbm, tokens.at[0]), "pet": (pet_hbm, tokens.at[1]),
        "gain_ct": (gain_ct_hbm, gain_ct), "gain_pet": (gain_pet_hbm, gain_pet),
        "wq": (wq_hbm, wq), "wk": (wk_hbm, wk), "wv": (wv_hbm, wv),
        "gain_ffn": (gain_ffn_hbm, gain_ffn),
        "wo": (wo_hbm, wo), "wup": (wup_hbm, wup), "wdown": (wdown_hbm, wdown),
        "anchor": (anchor_hbm, anchor_ref), "count": (count_hbm, count_ref),
        "anchor_row": (anchor_hbm, anchor_row), "count_row": (count_hbm, count_row),
        "wupc": (wupc_hbm, wupc), "wconv": (wconv_hbm, wconv),
    }
    loads = {
        name: pltpu.make_async_copy(src, dst, load_sem.at[i]) for i, (name, (src, dst)) in enumerate(plan.items())
    }
    names = list(plan)
    waited = set()

    def load(*which):
        for name in which:
            loads[name].start()

    def ready(*which):
        for name in which:
            if name not in waited:
                waited.add(name)
                loads[name].wait()

    load(*names[:7])

    barrier = pltpu.get_barrier_semaphore()

    def greet(target):
        pl.semaphore_signal(barrier, inc=1, device_id={"brick": target}, device_id_type=MESH)

    partner = position + 1 - 2 * core
    across = position - place + 2 - 2 * side

    def near(link):
        return partner if link == 1 else across + link - 2

    for link in range(1, 4):
        greet(near(link))
    for step in range(1, ring):
        greet(paired(deep, step) * 4 + kept)
    bridge = ((place == 0) & (deep > 0)) | ((place == 3) & (deep < ring - 1))

    @pl.when(bridge)
    def _():
        greet(position - 1 + 2 * core)

    load(*names[7:])
    entered = []

    def enter():
        if not entered:
            entered.append(1)
            pl.semaphore_wait(barrier, jnp.where(bridge, ring + 3, ring + 2))

    fine[...] = jnp.zeros_like(fine)
    halo_fine[...] = jnp.zeros_like(halo_fine)
    patches[...] = jnp.zeros_like(patches)

    def token_rows(s, m):
        return pl.ds(s * rows + m * window_tokens, window_tokens)

    def project(s):
        both = pl.ds(s * rows, rows)
        for m, gain in enumerate((gain_ct, gain_pet)):
            ready(("ct", "pet")[m], ("gain_ct", "gain_pet")[m])
            normed[token_rows(s, m), :] = rms_scale(tokens[m, s].astype(F32), gain[...].reshape(1, width))
        for name, weight, result in (("wq", wq, queries), ("wk", wk, keys), ("wv", wv, values)):
            ready(name)
            result[both, :] = matmul(normed[both, :], weight[...]).astype(BF16)

    low_half = lax.broadcasted_iota(jnp.int32, (1, SUB), 1) < DH
    low = jnp.where(low_half, 1.0, 0.0).astype(BF16)
    high = jnp.where(low_half, 0.0, 1.0).astype(BF16)
    ones = jnp.concatenate(
        [jnp.broadcast_to(low, (window_tokens, SUB)), jnp.broadcast_to(high, (window_tokens, SUB))], axis=0
    )

    def attention(s):
        for m in range(2):
            own, other = token_rows(s, m), token_rows(s, 1 - m)
            for pair in range(width // SUB):
                cols = pl.ds(pair * SUB, SUB)
                key = keys[other, cols]
                value = values[other, cols]
                scores = lax.dot_general(
                    queries[own, cols], jnp.concatenate([key * low, key * high], axis=0),
                    (((1,), (1,)), ((), ())), preferred_element_type=F32,
                )
                probs = []
                for h in range(2):
                    part = scores[:, h * window_tokens : (h + 1) * window_tokens]
                    row_max = jnp.max(part, axis=-1, keepdims=True)
                    probs.append(jnp.exp2((part - row_max) * (math.log2(math.e) / DH**0.5)).astype(BF16))
                heads = matmul(
                    jnp.concatenate(probs, axis=1),
                    jnp.concatenate([jnp.concatenate([value * low, value * high], axis=0), ones], axis=1),
                )
                mixed[own, cols] = (heads[:, :SUB] / heads[:, SUB:]).astype(BF16)

    def forward(s):
        both = pl.ds(s * rows, rows)
        ready("wo", "gain_ffn")
        for m in range(2):
            own = token_rows(s, m)
            mid = tokens[m, s].astype(F32) + matmul(mixed[own, :], wo[...])
            middle[own, :] = mid
            normed[own, :] = rms_scale(mid, gain_ffn[...].reshape(1, width))
        ready("wup")
        block = 512 if inner % 512 == 0 else inner
        for start in range(0, inner, block):
            cols = pl.ds(start, block)
            active = jax.nn.gelu(matmul(normed[both, :], wup[:, cols]), approximate=True)
            hidden[pl.ds(s * window_tokens, window_tokens), cols] = (
                active[:window_tokens] + active[window_tokens:]
            ).astype(BF16)

    def lower(s, c):
        ready("wdown")
        cols = pl.ds(c * cut, cut)
        total = (
            middle[token_rows(s, 0), cols] + middle[token_rows(s, 1), cols]
            + matmul(hidden[pl.ds(s * window_tokens, window_tokens), :], wdown[:, cols])
        )
        joined[s, c] = total.astype(BF16).reshape(WDEP, cells, cut)

    def remote(src, dst, send, recv, target):
        return pltpu.make_async_remote_copy(
            src_ref=src, dst_ref=dst, send_sem=send, recv_sem=recv,
            device_id={"brick": target}, device_id_type=MESH,
        )

    def near_copy(s, c, link):
        there = 1 if link == 1 else 2 + core
        return remote(
            share.at[s, c, link], got.at[s, c, there], send_x.at[s, c, link], recv_x.at[s, c, there], near(link)
        )

    def near_arrival(s, c, link):
        return remote(
            share.at[s, c, link], got.at[s, c, link], send_x.at[s, c, link], recv_x.at[s, c, link], near(link)
        )

    def depth_of(anchor, at):
        return jnp.bitwise_and(at - anchor, WDEP - 1)

    def send_near(s, c):
        anchor = anchor_ref[position * slots + s]
        for link in (2, 3, 1):
            target = near(link) % 4
            share[s, c, link] = joined[s, c, depth_of(anchor, target + 1 - 2 * (target % 2))]
            near_copy(s, c, link).start()
        share[s, c, 0] = joined[s, c, depth_of(anchor, kept)]

    def landed(s, link, z):
        slot = (near(link) if link else position) * slots + s
        anchor = anchor_ref[slot]
        depth = depth_of(anchor, kept)
        weight = count_ref[slot].astype(F32) * (1.0 / (2.0 * window_tokens)) * bell_at(depth)
        return jnp.where((anchor + depth) // 4 == z, weight, 0.0)

    def gather(s, c, z):
        total = None
        for link in range(4):
            block = (got if link else share)[s, c, link].astype(F32) * landed(s, link, z)
            total = block if total is None else total + block
        return total

    order = list(range(ring - 1, 0, -1)) + [0]

    def deep_copy(c, step):
        z = paired(deep, step)
        return remote(
            sum_z.at[c, z], got_z.at[c, deep], send_z.at[c, z], recv_z.at[c, deep], z * 4 + kept
        )

    def arrival(c, step):
        z = paired(deep, step)
        return z, remote(
            sum_z.at[c, z], got_z.at[c, z], send_z.at[c, z], recv_z.at[c, z], z * 4 + kept
        )

    last = slots - 1
    for s in range(slots):
        project(s)
        attention(s)
        forward(s)
        if s == 0:
            ready("anchor", "count")
            enter()
        for c in range(pieces):
            lower(s, c)
            if s == last:
                send_near(s, c)
        if s < last:
            for c in range(pieces):
                send_near(s, c)
    for s in range(last):
        for c in range(pieces):
            for link in range(1, 4):
                near_arrival(s, c, link).wait_recv()
            for step in order:
                z = paired(deep, step)
                block = gather(s, c, z)
                early[c, z] = block if s == 0 else early[c, z] + block

    def send_deep(c, steps):
        for step in steps:
            z = paired(deep, step)
            total = gather(last, c, z)
            if last:
                total = total + early[c, z]
            sum_z[c, z] = total.astype(BF16)
            deep_copy(c, step).start()

    near_steps = [1, 0]
    for c in range(pieces):
        for link in range(1, 4):
            near_arrival(last, c, link).wait_recv()
        send_deep(c, [step for step in order if step not in near_steps])
    for c in range(pieces):
        send_deep(c, [step for step in order if step in near_steps])
    ready("anchor_row", "count_row", "wupc", "wconv")
    row = (1, bricks * slots)
    denominator = jnp.sum(
        bell_at(position - anchor_row[...].reshape(row))
        * (count_row[...].reshape(row).astype(F32) * (1.0 / (2.0 * window_tokens))),
        axis=-1, keepdims=True,
    )
    inverse = 1.0 / jnp.maximum(denominator, 1.0)
    raised = None
    for c in range(pieces):
        numerator = None
        for step in range(ring):
            z, copy = arrival(c, step)
            copy.wait_recv()
            block = got_z[c, z].astype(F32)
            numerator = block if numerator is None else numerator + block
        feature = (numerator * inverse).astype(BF16)
        part = matmul(feature, wupc[pl.ds(c * cut, cut), :])
        raised = part if raised is None else raised + part
    raised = raised.astype(BF16).astype(F32)
    for a in range(2):
        for b in range(2):
            for c in range(2):
                at = ((a * 2 + b) * 2 + c) * channels
                for y in range(PY):
                    fine[a, 2 * y + b, pl.ds(8 + c, PX, stride=2), :] = raised[
                        y * PX : (y + 1) * PX, at : at + channels
                    ]
    for a in range(2):
        edge[a] = jnp.maximum(fine[a, :, 8 : 8 + 2 * PX, :], 0.0).astype(BF16)

    def edge_left():
        return remote(edge.at[0], got_edge.at[1], send_edge.at[0], recv_edge.at[1], position - 1)

    def edge_right():
        return remote(edge.at[1], got_edge.at[0], send_edge.at[1], recv_edge.at[0], position + 1)

    @pl.when(position > 0)
    def _():
        edge_left().start()

    @pl.when(position < bricks - 1)
    def _():
        edge_right().start()

    line = 2 * PX
    plane_rows = 2 * PY * line

    def fill(source, a, layer):
        for y in range(2 * PY):
            for dx in range(3):
                patches[layer, pl.ds((1 + y) * line, line), pl.ds(dx * channels, channels)] = jnp.maximum(
                    source[a, y, 7 + dx : 7 + dx + line, :], 0.0
                ).astype(BF16)

    def taps(layer, dz):
        acc = None
        for dy in range(3):
            term = matmul(
                patches[layer, pl.ds(dy * line, plane_rows), :],
                wconv[pl.ds((dz * 3 + dy) * 3 * channels, 3 * channels), :],
            )
            acc = term if acc is None else acc + term
        return acc

    fill(fine, 0, 1)
    fill(fine, 1, 2)
    upper = taps(1, 1) + taps(2, 2)
    lower_ = taps(1, 0) + taps(2, 1)

    for c in range(pieces):
        for s in range(slots):
            for link in range(1, 4):
                near_copy(s, c, link).wait_send()
        for step in range(ring):
            deep_copy(c, step).wait_send()

    @pl.when(position > 0)
    def _():
        edge_left().wait_send()
        remote(edge.at[1], got_edge.at[0], send_edge.at[1], recv_edge.at[0], position - 1).wait_recv()
        halo_fine[0, :, 8 : 8 + line, :] = got_edge[0].astype(F32)

    @pl.when(position < bricks - 1)
    def _():
        edge_right().wait_send()
        remote(edge.at[0], got_edge.at[1], send_edge.at[0], recv_edge.at[1], position + 1).wait_recv()
        halo_fine[1, :, 8 : 8 + line, :] = got_edge[1].astype(F32)

    fill(halo_fine, 0, 0)
    fill(halo_fine, 1, 3)
    upper = upper + taps(0, 0)
    lower_ = lower_ + taps(3, 2)
    for a, conv in enumerate((upper, lower_)):
        own = fine[a, :, 8 : 8 + line, :]
        out_ref[a] = (own + conv.reshape(own.shape)).astype(BF16)


def on_device(
    ct_win, pet_win, placed_anchor, placed_count, norm_ct, norm_pet, norm_ffn,
    w_query, w_key, w_value, w_out, w_up, w_down, w_upconv, w_conv,
):
    slots, window_tokens, width = ct_win.shape
    rows = 2 * slots * window_tokens
    bricks = lax.axis_size("brick")
    ring = bricks // 4
    cells = window_tokens // WDEP
    channels = w_conv.shape[1]
    line = 2 * PX
    cut = 256 if width % 256 == 0 else width
    pieces = width // cut
    dma = pltpu.SemaphoreType.DMA
    block = (cells, cut)

    def like(array):
        return pltpu.VMEM(array.shape, array.dtype)

    return pl.pallas_call(
        functools.partial(kernel, bricks),
        out_shape=pltpu.VMEM((2, 2 * PY, line, channels), BF16),
        in_specs=[pl.BlockSpec(memory_space=pl.ANY)] * 15,
        out_specs=pl.BlockSpec(memory_space=pltpu.VMEM),
        scratch_shapes=[
            pltpu.SMEM(placed_anchor.shape, jnp.int32), pltpu.SMEM(placed_count.shape, jnp.int32),
            like(placed_anchor), like(placed_count), like(norm_ct), like(norm_pet), like(norm_ffn),
            pltpu.VMEM((2,) + ct_win.shape, BF16),
            like(w_query), like(w_key), like(w_value), like(w_out), like(w_up), like(w_down),
            like(w_upconv), like(w_conv),
            pltpu.VMEM((rows, width), BF16),
            pltpu.VMEM((rows, width), BF16),
            pltpu.VMEM((rows, width), BF16),
            pltpu.VMEM((rows, width), BF16),
            pltpu.VMEM((rows, width), BF16),
            pltpu.VMEM((rows, width), F32),
            pltpu.VMEM((slots * window_tokens, w_up.shape[1]), BF16),
            pltpu.VMEM((slots, pieces, WDEP) + block, BF16),
            pltpu.VMEM((slots, pieces, 4) + block, BF16),
            pltpu.VMEM((slots, pieces, 4) + block, BF16),
            pltpu.VMEM((pieces, ring) + block, F32),
            pltpu.VMEM((pieces, ring) + block, BF16),
            pltpu.VMEM((pieces, ring) + block, BF16),
            pltpu.VMEM((2, 2 * PY, line + 16, channels), F32),
            pltpu.VMEM((2, 2 * PY, line + 16, channels), F32),
            pltpu.VMEM((2, 2 * PY, line, channels), BF16),
            pltpu.VMEM((2, 2 * PY, line, channels), BF16),
            pltpu.VMEM((4, (2 * PY + 2) * line, 3 * channels), BF16),
            dma((17,)), dma((slots, pieces, 4)), dma((slots, pieces, 4)),
            dma((pieces, ring)), dma((pieces, ring)), dma((2,)), dma((2,)),
        ],
        compiler_params=pltpu.CompilerParams(
            collective_id=0, has_side_effects=True, vmem_limit_bytes=62 * 1024 * 1024
        ),
        name="windows",
    )(
        placed_anchor, placed_count, norm_ct, norm_pet, norm_ffn,
        ct_win, pet_win, w_query, w_key, w_value, w_out, w_up, w_down, w_upconv, w_conv,
    )


def solution(mesh):
    split = P(("groups", "brick"), None, None)
    return jax.shard_map(
        on_device,
        mesh=mesh,
        in_specs=(split, split, P("groups"), P("groups")) + (P(),) * 11,
        out_specs=P(("groups", "brick"), None, None, None),
        check_vma=False,
    )
```

```python
import functools
import math

import jax
import jax.numpy as jnp
from jax import lax
from jax.experimental import pallas as pl
from jax.experimental.pallas import tpu as pltpu
from jax.sharding import PartitionSpec as P

DH = 64
PY = 4
PX = 8
WDEP = 4
SUB = 128

epsilon = 1e-06
F32 = jnp.float32
BF16 = jnp.bfloat16
MESH = pl.DeviceIdType.MESH


def rms_scale(inputs, gain_vec):
    mean_square = jnp.mean(inputs * inputs, axis=-1, keepdims=True)
    return (inputs * lax.rsqrt(mean_square + epsilon) * gain_vec).astype(BF16)


def matmul(left, right):
    return jnp.dot(left, right, preferred_element_type=F32)


def bell_at(depth):
    spread = WDEP / 4.0
    value = jnp.where(depth == depth, jnp.float32(0.0), jnp.float32(0.0))
    for i in range(WDEP):
        offset = i - (WDEP - 1) / 2.0
        value = jnp.where(depth == i, jnp.float32(math.exp(-offset * offset / (2.0 * spread * spread))), value)
    return value


def kernel(
    bricks,
    anchor_hbm, count_hbm, gain_ct_hbm, gain_pet_hbm, gain_ffn_hbm,
    ct_hbm, pet_hbm, wq_hbm, wk_hbm, wv_hbm, wo_hbm, wup_hbm, wdown_hbm, wupc_hbm, wconv_hbm,
    out_ref,
    anchor_ref, count_ref, anchor_row, count_row, gain_ct, gain_pet, gain_ffn,
    tokens, wq, wk, wv, wo, wup, wdown, wupc, wconv,
    normed, queries, keys, values, mixed, middle, hidden, joined,
    share, got, early, sum_z, got_z,
    fine, halo_fine, edge, got_edge, patches,
    load_sem, send_x, recv_x, send_z, recv_z, send_edge, recv_edge,
):
    position = lax.axis_index("brick")
    ring = bricks // 4
    place = position % 4
    core = position % 2
    side = (position // 2) % 2
    kept = place + 1 - 2 * core
    deep = position // 4

    slots, window_tokens, width = ct_hbm.shape
    rows = 2 * window_tokens
    cells = window_tokens // WDEP
    channels = wconv.shape[1]
    inner = wup.shape[1]
    pieces, cut = sum_z.shape[0], sum_z.shape[3]

    plan = {
        "ct": (ct_hbm, tokens.at[0]), "pet": (pet_hbm, tokens.at[1]),
        "gain_ct": (gain_ct_hbm, gain_ct), "gain_pet": (gain_pet_hbm, gain_pet),
        "wq": (wq_hbm, wq), "wk": (wk_hbm, wk), "wv": (wv_hbm, wv),
        "gain_ffn": (gain_ffn_hbm, gain_ffn),
        "wo": (wo_hbm, wo), "wup": (wup_hbm, wup), "wdown": (wdown_hbm, wdown),
        "anchor": (anchor_hbm, anchor_ref), "count": (count_hbm, count_ref),
        "anchor_row": (anchor_hbm, anchor_row), "count_row": (count_hbm, count_row),
        "wupc": (wupc_hbm, wupc), "wconv": (wconv_hbm, wconv),
    }
    loads = {
        name: pltpu.make_async_copy(src, dst, load_sem.at[i]) for i, (name, (src, dst)) in enumerate(plan.items())
    }
    names = list(plan)
    waited = set()

    def load(*which):
        for name in which:
            loads[name].start()

    def ready(*which):
        for name in which:
            if name not in waited:
                waited.add(name)
                loads[name].wait()

    load(*names[:7])

    barrier = pltpu.get_barrier_semaphore()

    def greet(target):
        pl.semaphore_signal(barrier, inc=1, device_id={"brick": target}, device_id_type=MESH)

    partner = position + 1 - 2 * core
    across = position - place + 2 - 2 * side

    def near(link):
        return partner if link == 1 else across + link - 2

    for link in range(1, 4):
        greet(near(link))
    for step in range(1, ring):
        greet(lax.rem(deep + step, ring) * 4 + kept)
    bridge = ((place == 0) & (deep > 0)) | ((place == 3) & (deep < ring - 1))

    @pl.when(bridge)
    def _():
        greet(position - 1 + 2 * core)

    load(*names[7:])
    entered = []

    def enter():
        if not entered:
            entered.append(1)
            pl.semaphore_wait(barrier, jnp.where(bridge, ring + 3, ring + 2))

    fine[...] = jnp.zeros_like(fine)
    halo_fine[...] = jnp.zeros_like(halo_fine)
    patches[...] = jnp.zeros_like(patches)

    def token_rows(s, m):
        return pl.ds(s * rows + m * window_tokens, window_tokens)

    def project(s):
        both = pl.ds(s * rows, rows)
        for m, gain in enumerate((gain_ct, gain_pet)):
            ready(("ct", "pet")[m], ("gain_ct", "gain_pet")[m])
            normed[token_rows(s, m), :] = rms_scale(tokens[m, s].astype(F32), gain[...].reshape(1, width))
        for name, weight, result in (("wq", wq, queries), ("wk", wk, keys), ("wv", wv, values)):
            ready(name)
            result[both, :] = matmul(normed[both, :], weight[...]).astype(BF16)

    low_half = lax.broadcasted_iota(jnp.int32, (1, SUB), 1) < DH
    low = jnp.where(low_half, 1.0, 0.0).astype(BF16)
    high = jnp.where(low_half, 0.0, 1.0).astype(BF16)
    ones = jnp.concatenate(
        [jnp.broadcast_to(low, (window_tokens, SUB)), jnp.broadcast_to(high, (window_tokens, SUB))], axis=0
    )

    def attention(s):
        for m in range(2):
            own, other = token_rows(s, m), token_rows(s, 1 - m)
            for pair in range(width // SUB):
                cols = pl.ds(pair * SUB, SUB)
                key = keys[other, cols]
                value = values[other, cols]
                scores = lax.dot_general(
                    queries[own, cols], jnp.concatenate([key * low, key * high], axis=0),
                    (((1,), (1,)), ((), ())), preferred_element_type=F32,
                )
                probs = []
                for h in range(2):
                    part = scores[:, h * window_tokens : (h + 1) * window_tokens]
                    row_max = jnp.max(part, axis=-1, keepdims=True)
                    probs.append(jnp.exp2((part - row_max) * (math.log2(math.e) / DH**0.5)).astype(BF16))
                heads = matmul(
                    jnp.concatenate(probs, axis=1),
                    jnp.concatenate([jnp.concatenate([value * low, value * high], axis=0), ones], axis=1),
                )
                mixed[own, cols] = (heads[:, :SUB] / heads[:, SUB:]).astype(BF16)

    def forward(s):
        both = pl.ds(s * rows, rows)
        ready("wo", "gain_ffn")
        for m in range(2):
            own = token_rows(s, m)
            mid = tokens[m, s].astype(F32) + matmul(mixed[own, :], wo[...])
            middle[own, :] = mid
            normed[own, :] = rms_scale(mid, gain_ffn[...].reshape(1, width))
        ready("wup")
        block = 512 if inner % 512 == 0 else inner
        for start in range(0, inner, block):
            cols = pl.ds(start, block)
            active = jax.nn.gelu(matmul(normed[both, :], wup[:, cols]), approximate=True)
            hidden[pl.ds(s * window_tokens, window_tokens), cols] = (
                active[:window_tokens] + active[window_tokens:]
            ).astype(BF16)

    def lower(s, c):
        ready("wdown")
        cols = pl.ds(c * cut, cut)
        total = (
            middle[token_rows(s, 0), cols] + middle[token_rows(s, 1), cols]
            + matmul(hidden[pl.ds(s * window_tokens, window_tokens), :], wdown[:, cols])
        )
        joined[s, c] = total.astype(BF16).reshape(WDEP, cells, cut)

    def remote(src, dst, send, recv, target):
        return pltpu.make_async_remote_copy(
            src_ref=src, dst_ref=dst, send_sem=send, recv_sem=recv,
            device_id={"brick": target}, device_id_type=MESH,
        )

    def near_pair(s, link, there, c):
        pick = (lambda ref, at: ref.at[s, at]) if c is None else (lambda ref, at: ref.at[s, at, c])
        c = 0 if c is None else c
        return remote(
            pick(share, link), pick(got, there), send_x.at[s, link, c], recv_x.at[s, there, c], near(link)
        )

    def near_copy(s, link, c=None):
        return near_pair(s, link, 1 if link == 1 else 2 + core, c)

    def near_arrival(s, link, c=None):
        return near_pair(s, link, link, c)

    def depth_of(anchor, at):
        return jnp.bitwise_and(at - anchor, WDEP - 1)

    def fetch(s, c, link, anchor):
        target = near(link) % 4 if link else partner % 4
        own = target + 1 - 2 * (target % 2) if link else target
        share[s, link, c] = joined[s, c, depth_of(anchor, own)]

    def source(s, link):
        slot = (near(link) if link else position) * slots + s
        anchor = anchor_ref[slot]
        depth = depth_of(anchor, kept)
        weight = count_ref[slot].astype(F32) * (1.0 / (2.0 * window_tokens)) * bell_at(depth)
        return (anchor + depth) // 4, weight

    def gather(s, c, z, sources):
        total = None
        for link, (where, weight) in enumerate(sources):
            block = (got if link else share)[s, link, c].astype(F32) * jnp.where(where == z, weight, 0.0)
            total = block if total is None else total + block
        return total

    def deep_pair(c, z, there):
        return remote(
            sum_z.at[c, z], got_z.at[c, there], send_z.at[c, z], recv_z.at[c, there], z * 4 + kept
        )

    last = slots - 1
    for s in range(slots):
        project(s)
        attention(s)
        forward(s)
        if s == 0:
            ready("anchor", "count")
            enter()
        anchor = anchor_ref[position * slots + s]
        if s < last:
            for c in range(pieces):
                lower(s, c)
            for link in (2, 3, 1):
                for c in range(pieces):
                    fetch(s, c, link, anchor)
                near_copy(s, link).start()
            for c in range(pieces):
                fetch(s, c, 0, anchor)
        else:
            for c in range(pieces):
                lower(s, c)
                for link in (2, 3, 1):
                    fetch(s, c, link, anchor)
                    near_copy(s, link, c).start()
                fetch(s, c, 0, anchor)
    for s in range(last):
        sources = [source(s, link) for link in range(4)]
        for link in range(1, 4):
            near_arrival(s, link).wait_recv()
        for c in range(pieces):
            for z in range(ring):
                block = gather(s, c, z, sources)
                early[c, z] = block if s == 0 else early[c, z] + block
    sources = [source(last, link) for link in range(4)]

    def send_deep(c, planes):
        for z in planes:
            total = gather(last, c, z, sources)
            if last:
                total = total + early[c, z]
            sum_z[c, z] = total.astype(BF16)
            deep_pair(c, z, deep).start()

    soon = ring // 2
    for c in range(pieces):
        for link in range(1, 4):
            near_arrival(last, link, c).wait_recv()
        send_deep(c, range(soon))
    for z in range(soon, ring):
        for c in range(pieces):
            send_deep(c, [z])
    ready("anchor_row", "count_row", "wupc", "wconv")
    row = (1, bricks * slots)
    denominator = jnp.sum(
        bell_at(position - anchor_row[...].reshape(row))
        * (count_row[...].reshape(row).astype(F32) * (1.0 / (2.0 * window_tokens))),
        axis=-1, keepdims=True,
    )
    inverse = 1.0 / jnp.maximum(denominator, 1.0)
    raised = None
    for c in range(pieces):
        numerator = None
        for z in range(ring):
            deep_pair(c, z, z).wait_recv()
            block = got_z[c, z].astype(F32)
            numerator = block if numerator is None else numerator + block
        feature = (numerator * inverse).astype(BF16)
        part = matmul(feature, wupc[pl.ds(c * cut, cut), :])
        raised = part if raised is None else raised + part
    raised = raised.astype(BF16).astype(F32)
    for a in range(2):
        for b in range(2):
            for c in range(2):
                at = ((a * 2 + b) * 2 + c) * channels
                for y in range(PY):
                    fine[a, 2 * y + b, pl.ds(8 + c, PX, stride=2), :] = raised[
                        y * PX : (y + 1) * PX, at : at + channels
                    ]
    for a in range(2):
        edge[a] = jnp.maximum(fine[a, :, 8 : 8 + 2 * PX, :], 0.0).astype(BF16)

    def edge_left():
        return remote(edge.at[0], got_edge.at[1], send_edge.at[0], recv_edge.at[1], position - 1)

    def edge_right():
        return remote(edge.at[1], got_edge.at[0], send_edge.at[1], recv_edge.at[0], position + 1)

    @pl.when(position > 0)
    def _():
        edge_left().start()

    @pl.when(position < bricks - 1)
    def _():
        edge_right().start()

    line = 2 * PX
    plane_rows = 2 * PY * line

    def fill(source, a, layer):
        for y in range(2 * PY):
            for dx in range(3):
                patches[layer, pl.ds((1 + y) * line, line), pl.ds(dx * channels, channels)] = jnp.maximum(
                    source[a, y, 7 + dx : 7 + dx + line, :], 0.0
                ).astype(BF16)

    def taps(layer, dz):
        acc = None
        for dy in range(3):
            term = matmul(
                patches[layer, pl.ds(dy * line, plane_rows), :],
                wconv[pl.ds((dz * 3 + dy) * 3 * channels, 3 * channels), :],
            )
            acc = term if acc is None else acc + term
        return acc

    fill(fine, 0, 1)
    fill(fine, 1, 2)
    upper = taps(1, 1) + taps(2, 2)
    lower_ = taps(1, 0) + taps(2, 1)

    for link in range(1, 4):
        for s in range(last):
            near_copy(s, link).wait_send()
        for c in range(pieces):
            near_copy(last, link, c).wait_send()
    for c in range(pieces):
        for z in range(ring):
            deep_pair(c, z, deep).wait_send()

    @pl.when(position > 0)
    def _():
        edge_left().wait_send()
        remote(edge.at[1], got_edge.at[0], send_edge.at[1], recv_edge.at[0], position - 1).wait_recv()
        halo_fine[0, :, 8 : 8 + line, :] = got_edge[0].astype(F32)

    @pl.when(position < bricks - 1)
    def _():
        edge_right().wait_send()
        remote(edge.at[0], got_edge.at[1], send_edge.at[0], recv_edge.at[1], position + 1).wait_recv()
        halo_fine[1, :, 8 : 8 + line, :] = got_edge[1].astype(F32)

    fill(halo_fine, 0, 0)
    fill(halo_fine, 1, 3)
    upper = upper + taps(0, 0)
    lower_ = lower_ + taps(3, 2)
    for a, conv in enumerate((upper, lower_)):
        own = fine[a, :, 8 : 8 + line, :]
        out_ref[a] = (own + conv.reshape(own.shape)).astype(BF16)


def on_device(
    ct_win, pet_win, placed_anchor, placed_count, norm_ct, norm_pet, norm_ffn,
    w_query, w_key, w_value, w_out, w_up, w_down, w_upconv, w_conv,
):
    slots, window_tokens, width = ct_win.shape
    rows = 2 * slots * window_tokens
    bricks = lax.axis_size("brick")
    ring = bricks // 4
    cells = window_tokens // WDEP
    channels = w_conv.shape[1]
    line = 2 * PX
    cut = 256 if width % 256 == 0 else width
    pieces = width // cut
    dma = pltpu.SemaphoreType.DMA
    block = (cells, cut)

    def like(array):
        return pltpu.VMEM(array.shape, array.dtype)

    return pl.pallas_call(
        functools.partial(kernel, bricks),
        out_shape=pltpu.VMEM((2, 2 * PY, line, channels), BF16),
        in_specs=[pl.BlockSpec(memory_space=pl.ANY)] * 15,
        out_specs=pl.BlockSpec(memory_space=pltpu.VMEM),
        scratch_shapes=[
            pltpu.SMEM(placed_anchor.shape, jnp.int32), pltpu.SMEM(placed_count.shape, jnp.int32),
            like(placed_anchor), like(placed_count), like(norm_ct), like(norm_pet), like(norm_ffn),
            pltpu.VMEM((2,) + ct_win.shape, BF16),
            like(w_query), like(w_key), like(w_value), like(w_out), like(w_up), like(w_down),
            like(w_upconv), like(w_conv),
            pltpu.VMEM((rows, width), BF16),
            pltpu.VMEM((rows, width), BF16),
            pltpu.VMEM((rows, width), BF16),
            pltpu.VMEM((rows, width), BF16),
            pltpu.VMEM((rows, width), BF16),
            pltpu.VMEM((rows, width), F32),
            pltpu.VMEM((slots * window_tokens, w_up.shape[1]), BF16),
            pltpu.VMEM((slots, pieces, WDEP) + block, BF16),
            pltpu.VMEM((slots, 4, pieces) + block, BF16),
            pltpu.VMEM((slots, 4, pieces) + block, BF16),
            pltpu.VMEM((pieces, ring) + block, F32),
            pltpu.VMEM((pieces, ring) + block, BF16),
            pltpu.VMEM((pieces, ring) + block, BF16),
            pltpu.VMEM((2, 2 * PY, line + 16, channels), F32),
            pltpu.VMEM((2, 2 * PY, line + 16, channels), F32),
            pltpu.VMEM((2, 2 * PY, line, channels), BF16),
            pltpu.VMEM((2, 2 * PY, line, channels), BF16),
            pltpu.VMEM((4, (2 * PY + 2) * line, 3 * channels), BF16),
            dma((17,)), dma((slots, 4, pieces)), dma((slots, 4, pieces)),
            dma((pieces, ring)), dma((pieces, ring)), dma((2,)), dma((2,)),
        ],
        compiler_params=pltpu.CompilerParams(
            collective_id=0, has_side_effects=True, vmem_limit_bytes=62 * 1024 * 1024
        ),
        name="windows",
    )(
        placed_anchor, placed_count, norm_ct, norm_pet, norm_ffn,
        ct_win, pet_win, w_query, w_key, w_value, w_out, w_up, w_down, w_upconv, w_conv,
    )


def solution(mesh):
    split = P(("groups", "brick"), None, None)
    return jax.shard_map(
        on_device,
        mesh=mesh,
        in_specs=(split, split, P("groups"), P("groups")) + (P(),) * 11,
        out_specs=P(("groups", "brick"), None, None, None),
        check_vma=False,
    )
```

```python
import functools
import math

import jax
import jax.numpy as jnp
from jax import lax
from jax.experimental import pallas as pl
from jax.experimental.pallas import tpu as pltpu
from jax.sharding import PartitionSpec as P

DH = 64
PY = 4
PX = 8
WDEP = 4
SUB = 128

epsilon = 1e-06
F32 = jnp.float32
BF16 = jnp.bfloat16
MESH = pl.DeviceIdType.MESH


def rms_scale(inputs, gain_vec):
    mean_square = jnp.mean(inputs * inputs, axis=-1, keepdims=True)
    return (inputs * lax.rsqrt(mean_square + epsilon) * gain_vec).astype(BF16)


def matmul(left, right):
    return jnp.dot(left, right, preferred_element_type=F32)


def bell_at(depth):
    spread = WDEP / 4.0
    value = jnp.where(depth == depth, jnp.float32(0.0), jnp.float32(0.0))
    for i in range(WDEP):
        offset = i - (WDEP - 1) / 2.0
        value = jnp.where(depth == i, jnp.float32(math.exp(-offset * offset / (2.0 * spread * spread))), value)
    return value


def kernel(
    bricks,
    anchor_hbm, count_hbm, gain_ct_hbm, gain_pet_hbm, gain_ffn_hbm,
    ct_hbm, pet_hbm, wq_hbm, wk_hbm, wv_hbm, wo_hbm, wup_hbm, wdown_hbm, wupc_hbm, wconv_hbm,
    out_ref,
    anchor_ref, count_ref, anchor_row, count_row, gain_ct, gain_pet, gain_ffn,
    tokens, wqkv, wo, wup, wdown, wupc, wconv,
    normed, projected, mixed, middle, hidden, joined,
    share, got, early, sum_z, got_z,
    fine, halo_fine, edge, got_edge, patches, conv,
    load_sem, send_x, recv_x, send_z, recv_z, send_edge, recv_edge,
):
    position = lax.axis_index("brick")
    ring = bricks // 4
    place = position % 4
    core = position % 2
    side = (position // 2) % 2
    kept = place + 1 - 2 * core
    deep = position // 4

    slots, window_tokens, width = ct_hbm.shape
    rows = 2 * window_tokens
    cells = window_tokens // WDEP
    channels = wconv.shape[1]
    inner = wup.shape[1]
    pieces, cut = sum_z.shape[0], sum_z.shape[3]

    plan = {
        "ct": (ct_hbm, tokens.at[0]), "pet": (pet_hbm, tokens.at[1]),
        "gain_ct": (gain_ct_hbm, gain_ct), "gain_pet": (gain_pet_hbm, gain_pet),
        "wq": (wq_hbm, wqkv.at[:, pl.ds(0, width)]),
        "wk": (wk_hbm, wqkv.at[:, pl.ds(width, width)]),
        "wv": (wv_hbm, wqkv.at[:, pl.ds(2 * width, width)]),
        "gain_ffn": (gain_ffn_hbm, gain_ffn),
        "wo": (wo_hbm, wo), "wup": (wup_hbm, wup), "wdown": (wdown_hbm, wdown),
        "anchor": (anchor_hbm, anchor_ref), "count": (count_hbm, count_ref),
        "anchor_row": (anchor_hbm, anchor_row), "count_row": (count_hbm, count_row),
        "wupc": (wupc_hbm, wupc), "wconv": (wconv_hbm, wconv),
    }
    loads = {
        name: pltpu.make_async_copy(src, dst, load_sem.at[i]) for i, (name, (src, dst)) in enumerate(plan.items())
    }
    names = list(plan)
    waited = set()

    def load(*which):
        for name in which:
            loads[name].start()

    def ready(*which):
        for name in which:
            if name not in waited:
                waited.add(name)
                loads[name].wait()

    load(*names[:7])

    barrier = pltpu.get_barrier_semaphore()

    def greet(target):
        pl.semaphore_signal(barrier, inc=1, device_id={"brick": target}, device_id_type=MESH)

    partner = position + 1 - 2 * core
    across = position - place + 2 - 2 * side

    def near(link):
        return partner if link == 1 else across + link - 2

    for link in range(1, 4):
        greet(near(link))
    for step in range(1, ring):
        greet(lax.rem(deep + step, ring) * 4 + kept)
    bridge = ((place == 0) & (deep > 0)) | ((place == 3) & (deep < ring - 1))

    @pl.when(bridge)
    def _():
        greet(position - 1 + 2 * core)

    load(*names[7:])
    entered = []

    def enter():
        if not entered:
            entered.append(1)
            pl.semaphore_wait(barrier, jnp.where(bridge, ring + 3, ring + 2))

    fine[...] = jnp.zeros_like(fine)
    halo_fine[...] = jnp.zeros_like(halo_fine)
    patches[...] = jnp.zeros_like(patches)

    def token_rows(s, m):
        return pl.ds(s * rows + m * window_tokens, window_tokens)

    def normalize(s):
        for m, gain in enumerate((gain_ct, gain_pet)):
            ready(("ct", "pet")[m], ("gain_ct", "gain_pet")[m])
            normed[token_rows(s, m), :] = rms_scale(tokens[m, s].astype(F32), gain[...].reshape(1, width))

    def project(s):
        both = pl.ds(s * rows, rows)
        if s == 0:
            for i, name in enumerate(("wq", "wk", "wv")):
                ready(name)
                cols = pl.ds(i * width, width)
                projected[both, cols] = matmul(normed[both, :], wqkv[:, cols]).astype(BF16)
        else:
            projected[both, :] = matmul(normed[both, :], wqkv[...]).astype(BF16)

    low_half = lax.broadcasted_iota(jnp.int32, (1, SUB), 1) < DH
    low = jnp.where(low_half, 1.0, 0.0).astype(BF16)
    high = jnp.where(low_half, 0.0, 1.0).astype(BF16)
    ones = jnp.concatenate(
        [jnp.broadcast_to(low, (window_tokens, SUB)), jnp.broadcast_to(high, (window_tokens, SUB))], axis=0
    )

    def attention(s):
        for m in range(2):
            own, other = token_rows(s, m), token_rows(s, 1 - m)
            for pair in range(width // SUB):
                cols = pl.ds(pair * SUB, SUB)
                key = projected[other, pl.ds(width + pair * SUB, SUB)]
                value = projected[other, pl.ds(2 * width + pair * SUB, SUB)]
                scores = lax.dot_general(
                    projected[own, cols], jnp.concatenate([key * low, key * high], axis=0),
                    (((1,), (1,)), ((), ())), preferred_element_type=F32,
                )
                probs = []
                for h in range(2):
                    part = scores[:, h * window_tokens : (h + 1) * window_tokens]
                    row_max = jnp.max(part, axis=-1, keepdims=True)
                    probs.append(jnp.exp2((part - row_max) * (math.log2(math.e) / DH**0.5)).astype(BF16))
                heads = matmul(
                    jnp.concatenate(probs, axis=1),
                    jnp.concatenate([jnp.concatenate([value * low, value * high], axis=0), ones], axis=1),
                )
                mixed[own, cols] = (heads[:, :SUB] / heads[:, SUB:]).astype(BF16)

    def forward(s):
        both = pl.ds(s * rows, rows)
        ready("wo", "gain_ffn")
        for m in range(2):
            own = token_rows(s, m)
            mid = tokens[m, s].astype(F32) + matmul(mixed[own, :], wo[...])
            middle[own, :] = mid
            normed[own, :] = rms_scale(mid, gain_ffn[...].reshape(1, width))
        ready("wup")
        block = 512 if inner % 512 == 0 else inner
        for start in range(0, inner, block):
            cols = pl.ds(start, block)
            active = jax.nn.gelu(matmul(normed[both, :], wup[:, cols]), approximate=True)
            hidden[pl.ds(s * window_tokens, window_tokens), cols] = (
                active[:window_tokens] + active[window_tokens:]
            ).astype(BF16)

    def lower(s, c):
        ready("wdown")
        cols = pl.ds(c * cut, cut)
        total = (
            middle[token_rows(s, 0), cols] + middle[token_rows(s, 1), cols]
            + matmul(hidden[pl.ds(s * window_tokens, window_tokens), :], wdown[:, cols])
        )
        joined[s, c] = total.astype(BF16).reshape(WDEP, cells, cut)

    def remote(src, dst, send, recv, target):
        return pltpu.make_async_remote_copy(
            src_ref=src, dst_ref=dst, send_sem=send, recv_sem=recv,
            device_id={"brick": target}, device_id_type=MESH,
        )

    def near_pair(s, link, there, c):
        pick = (lambda ref, at: ref.at[s, at]) if c is None else (lambda ref, at: ref.at[s, at, c])
        c = 0 if c is None else c
        return remote(
            pick(share, link), pick(got, there), send_x.at[s, link, c], recv_x.at[s, there, c], near(link)
        )

    def near_copy(s, link, c=None):
        return near_pair(s, link, 1 if link == 1 else 2 + core, c)

    def near_arrival(s, link, c=None):
        return near_pair(s, link, link, c)

    def depth_of(anchor, at):
        return jnp.bitwise_and(at - anchor, WDEP - 1)

    def fetch(s, c, link, anchor):
        target = near(link) % 4 if link else partner % 4
        own = target + 1 - 2 * (target % 2) if link else target
        share[s, link, c] = joined[s, c, depth_of(anchor, own)]

    def source(s, link):
        slot = (near(link) if link else position) * slots + s
        anchor = anchor_ref[slot]
        depth = depth_of(anchor, kept)
        weight = count_ref[slot].astype(F32) * (1.0 / (2.0 * window_tokens)) * bell_at(depth)
        return (anchor + depth) // 4, weight

    def gather(s, c, z, sources):
        total = None
        for link, (where, weight) in enumerate(sources):
            block = (got if link else share)[s, link, c].astype(F32) * jnp.where(where == z, weight, 0.0)
            total = block if total is None else total + block
        return total

    def deep_pair(c, z, there):
        return remote(
            sum_z.at[c, z], got_z.at[c, there], send_z.at[c, z], recv_z.at[c, there], z * 4 + kept
        )

    last = slots - 1
    for s in range(slots):
        normalize(s)
    for s in range(slots):
        project(s)
        attention(s)
        forward(s)
        if s == 0:
            ready("anchor", "count")
            enter()
        anchor = anchor_ref[position * slots + s]
        if s < last:
            for c in range(pieces):
                lower(s, c)
            for link in (1, 2, 3):
                for c in range(pieces):
                    fetch(s, c, link, anchor)
                near_copy(s, link).start()
            for c in range(pieces):
                fetch(s, c, 0, anchor)
        else:
            for c in range(pieces):
                lower(s, c)
                for link in (1, 2, 3):
                    fetch(s, c, link, anchor)
                    near_copy(s, link, c).start()
                fetch(s, c, 0, anchor)
    for s in range(last):
        sources = [source(s, link) for link in range(4)]
        for link in range(1, 4):
            near_arrival(s, link).wait_recv()
        for c in range(pieces):
            for z in range(ring):
                block = gather(s, c, z, sources)
                early[c, z] = block if s == 0 else early[c, z] + block
    sources = [source(last, link) for link in range(4)]

    def send_deep(c, planes):
        for z in planes:
            total = gather(last, c, z, sources)
            if last:
                total = total + early[c, z]
            sum_z[c, z] = total.astype(BF16)
            deep_pair(c, z, deep).start()

    soon = ring // 2
    for c in range(pieces):
        for link in range(1, 4):
            near_arrival(last, link, c).wait_recv()
        send_deep(c, range(soon))
    for z in range(soon, ring):
        for c in range(pieces):
            send_deep(c, [z])
    ready("anchor_row", "count_row", "wupc", "wconv")
    row = (1, bricks * slots)
    denominator = jnp.sum(
        bell_at(position - anchor_row[...].reshape(row))
        * (count_row[...].reshape(row).astype(F32) * (1.0 / (2.0 * window_tokens))),
        axis=-1, keepdims=True,
    )
    inverse = 1.0 / jnp.maximum(denominator, 1.0)
    def edge_left():
        return remote(edge.at[0], got_edge.at[1], send_edge.at[0], recv_edge.at[1], position - 1)

    def edge_right():
        return remote(edge.at[1], got_edge.at[0], send_edge.at[1], recv_edge.at[0], position + 1)

    features = []
    for c in range(pieces):
        numerator = None
        for z in range(ring):
            deep_pair(c, z, z).wait_recv()
            block = got_z[c, z].astype(F32)
            numerator = block if numerator is None else numerator + block
        features.append((numerator * inverse).astype(BF16))

    for a, has_side, send in ((0, position > 0, edge_left), (1, position < bricks - 1, edge_right)):
        raised = None
        for c in range(pieces):
            part = matmul(features[c], wupc[pl.ds(c * cut, cut), pl.ds(a * 4 * channels, 4 * channels)])
            raised = part if raised is None else raised + part
        raised = raised.astype(BF16).astype(F32)
        for b in range(2):
            for c in range(2):
                at = (b * 2 + c) * channels
                for y in range(PY):
                    fine[a, 2 * y + b, pl.ds(8 + c, PX, stride=2), :] = raised[
                        y * PX : (y + 1) * PX, at : at + channels
                    ]
        edge[a] = jnp.maximum(fine[a, :, 8 : 8 + 2 * PX, :], 0.0).astype(BF16)

        @pl.when(has_side)
        def _():
            send().start()

    line = 2 * PX
    plane_rows = 2 * PY * line

    def fill(source, a, layer):
        for y in range(2 * PY):
            for dx in range(3):
                patches[layer, pl.ds((1 + y) * line, line), pl.ds(dx * channels, channels)] = jnp.maximum(
                    source[a, y, 7 + dx : 7 + dx + line, :], 0.0
                ).astype(BF16)

    def taps(layer, dz):
        acc = None
        for dy in range(3):
            term = matmul(
                patches[layer, pl.ds(dy * line, plane_rows), :],
                wconv[pl.ds((dz * 3 + dy) * 3 * channels, 3 * channels), :],
            )
            acc = term if acc is None else acc + term
        return acc

    fill(fine, 0, 1)
    fill(fine, 1, 2)
    upper = taps(1, 1) + taps(2, 2)
    lower_ = taps(1, 0) + taps(2, 1)

    for link in range(1, 4):
        for s in range(last):
            near_copy(s, link).wait_send()
        for c in range(pieces):
            near_copy(last, link, c).wait_send()
    for c in range(pieces):
        for z in range(ring):
            deep_pair(c, z, deep).wait_send()

    conv[0] = upper
    conv[1] = lower_

    def halo(end):
        @pl.when((position > 0) if end == 0 else (position < bricks - 1))
        def _():
            if end == 0:
                remote(edge.at[1], got_edge.at[0], send_edge.at[1], recv_edge.at[0], position - 1).wait_recv()
            else:
                remote(edge.at[0], got_edge.at[1], send_edge.at[0], recv_edge.at[1], position + 1).wait_recv()
            halo_fine[end, :, 8 : 8 + line, :] = got_edge[end].astype(F32)
            fill(halo_fine, end, 3 * end)
            conv[end] = conv[end] + taps(3 * end, 2 * end)

    @pl.when(core == 0)
    def _():
        halo(1)
        halo(0)

    @pl.when(core == 1)
    def _():
        halo(0)
        halo(1)

    @pl.when(position > 0)
    def _():
        edge_left().wait_send()

    @pl.when(position < bricks - 1)
    def _():
        edge_right().wait_send()

    for a in range(2):
        own = fine[a, :, 8 : 8 + line, :]
        out_ref[a] = (own + conv[a].reshape(own.shape)).astype(BF16)


def on_device(
    ct_win, pet_win, placed_anchor, placed_count, norm_ct, norm_pet, norm_ffn,
    w_query, w_key, w_value, w_out, w_up, w_down, w_upconv, w_conv,
):
    slots, window_tokens, width = ct_win.shape
    rows = 2 * slots * window_tokens
    bricks = lax.axis_size("brick")
    ring = bricks // 4
    cells = window_tokens // WDEP
    channels = w_conv.shape[1]
    line = 2 * PX
    cut = 256 if width % 256 == 0 else width
    pieces = width // cut
    dma = pltpu.SemaphoreType.DMA
    block = (cells, cut)

    def like(array):
        return pltpu.VMEM(array.shape, array.dtype)

    return pl.pallas_call(
        functools.partial(kernel, bricks),
        out_shape=pltpu.VMEM((2, 2 * PY, line, channels), BF16),
        in_specs=[pl.BlockSpec(memory_space=pl.ANY)] * 15,
        out_specs=pl.BlockSpec(memory_space=pltpu.VMEM),
        scratch_shapes=[
            pltpu.SMEM(placed_anchor.shape, jnp.int32), pltpu.SMEM(placed_count.shape, jnp.int32),
            like(placed_anchor), like(placed_count), like(norm_ct), like(norm_pet), like(norm_ffn),
            pltpu.VMEM((2,) + ct_win.shape, BF16),
            pltpu.VMEM((width, 3 * width), BF16), like(w_out), like(w_up), like(w_down),
            like(w_upconv), like(w_conv),
            pltpu.VMEM((rows, width), BF16),
            pltpu.VMEM((rows, 3 * width), BF16),
            pltpu.VMEM((rows, width), BF16),
            pltpu.VMEM((rows, width), F32),
            pltpu.VMEM((slots * window_tokens, w_up.shape[1]), BF16),
            pltpu.VMEM((slots, pieces, WDEP) + block, BF16),
            pltpu.VMEM((slots, 4, pieces) + block, BF16),
            pltpu.VMEM((slots, 4, pieces) + block, BF16),
            pltpu.VMEM((pieces, ring) + block, F32),
            pltpu.VMEM((pieces, ring) + block, BF16),
            pltpu.VMEM((pieces, ring) + block, BF16),
            pltpu.VMEM((2, 2 * PY, line + 16, channels), F32),
            pltpu.VMEM((2, 2 * PY, line + 16, channels), F32),
            pltpu.VMEM((2, 2 * PY, line, channels), BF16),
            pltpu.VMEM((2, 2 * PY, line, channels), BF16),
            pltpu.VMEM((4, (2 * PY + 2) * line, 3 * channels), BF16),
            pltpu.VMEM((2, 2 * PY * line, channels), F32),
            dma((17,)), dma((slots, 4, pieces)), dma((slots, 4, pieces)),
            dma((pieces, ring)), dma((pieces, ring)), dma((2,)), dma((2,)),
        ],
        compiler_params=pltpu.CompilerParams(
            collective_id=0, has_side_effects=True, vmem_limit_bytes=62 * 1024 * 1024
        ),
        name="windows",
    )(
        placed_anchor, placed_count, norm_ct, norm_pet, norm_ffn,
        ct_win, pet_win, w_query, w_key, w_value, w_out, w_up, w_down, w_upconv, w_conv,
    )


def solution(mesh):
    split = P(("groups", "brick"), None, None)
    return jax.shard_map(
        on_device,
        mesh=mesh,
        in_specs=(split, split, P("groups"), P("groups")) + (P(),) * 11,
        out_specs=P(("groups", "brick"), None, None, None),
        check_vma=False,
    )
```

```python
import functools
import math

import jax
import jax.numpy as jnp
from jax import lax
from jax.experimental import pallas as pl
from jax.experimental.pallas import tpu as pltpu
from jax.sharding import PartitionSpec as P

DH = 64
PY = 4
PX = 8
WDEP = 4
SUB = 128

epsilon = 1e-06
GELU_ONE = math.sqrt(2.0 / math.pi)
GELU_THREE = 0.044715 * GELU_ONE
F32 = jnp.float32
BF16 = jnp.bfloat16
MESH = pl.DeviceIdType.MESH


def rms_scale(inputs, gain_vec):
    mean_square = jnp.mean(inputs * inputs, axis=-1, keepdims=True)
    return (inputs * lax.rsqrt(mean_square + epsilon) * gain_vec).astype(BF16)


def matmul(left, right):
    return jnp.dot(left, right, preferred_element_type=F32)


def bell_at(depth):
    spread = WDEP / 4.0
    value = jnp.where(depth == depth, jnp.float32(0.0), jnp.float32(0.0))
    for i in range(WDEP):
        offset = i - (WDEP - 1) / 2.0
        value = jnp.where(depth == i, jnp.float32(math.exp(-offset * offset / (2.0 * spread * spread))), value)
    return value


def kernel(
    bricks,
    anchor_hbm, count_hbm, gain_ct_hbm, gain_pet_hbm, gain_ffn_hbm,
    ct_hbm, pet_hbm, wq_hbm, wk_hbm, wv_hbm, wo_hbm, wup_hbm, wdown_hbm, wupc_hbm, wconv_hbm,
    out_ref,
    anchor_ref, count_ref, anchor_row, count_row, gain_ct, gain_pet, gain_ffn,
    tokens, wqkv, wo, wup, wdown, wupc, wconv,
    normed, projected, mixed, middle, hidden, joined,
    share, got, early, sum_z, got_z,
    fine, halo_fine, edge, got_edge, patches, conv,
    load_sem, send_x, recv_x, send_z, recv_z, send_edge, recv_edge,
):
    position = lax.axis_index("brick")
    ring = bricks // 4
    place = position % 4
    core = position % 2
    side = (position // 2) % 2
    kept = place + 1 - 2 * core
    deep = position // 4

    slots, window_tokens, width = ct_hbm.shape
    rows = 2 * window_tokens
    cells = window_tokens // WDEP
    channels = wconv.shape[1]
    inner = wup.shape[1]
    pieces, cut = sum_z.shape[0], sum_z.shape[3]

    plan = {
        "ct": (ct_hbm, tokens.at[0]), "pet": (pet_hbm, tokens.at[1]),
        "gain_ct": (gain_ct_hbm, gain_ct), "gain_pet": (gain_pet_hbm, gain_pet),
        "wq": (wq_hbm, wqkv.at[:, pl.ds(0, width)]),
        "wk": (wk_hbm, wqkv.at[:, pl.ds(width, width)]),
        "wv": (wv_hbm, wqkv.at[:, pl.ds(2 * width, width)]),
        "gain_ffn": (gain_ffn_hbm, gain_ffn),
        "wo": (wo_hbm, wo), "wup": (wup_hbm, wup), "wdown": (wdown_hbm, wdown),
        "anchor": (anchor_hbm, anchor_ref), "count": (count_hbm, count_ref),
        "anchor_row": (anchor_hbm, anchor_row), "count_row": (count_hbm, count_row),
        "wupc": (wupc_hbm, wupc), "wconv": (wconv_hbm, wconv),
    }
    loads = {
        name: pltpu.make_async_copy(src, dst, load_sem.at[i]) for i, (name, (src, dst)) in enumerate(plan.items())
    }
    names = list(plan)
    waited = set()

    def load(*which):
        for name in which:
            loads[name].start()

    def ready(*which):
        for name in which:
            if name not in waited:
                waited.add(name)
                loads[name].wait()

    load(*names[:7])

    barrier = pltpu.get_barrier_semaphore()

    def greet(target):
        pl.semaphore_signal(barrier, inc=1, device_id={"brick": target}, device_id_type=MESH)

    partner = position + 1 - 2 * core
    across = position - place + 2 - 2 * side

    def near(link):
        return partner if link == 1 else across + link - 2

    for link in range(1, 4):
        greet(near(link))
    for step in range(1, ring):
        greet(lax.rem(deep + step, ring) * 4 + kept)
    bridge = ((place == 0) & (deep > 0)) | ((place == 3) & (deep < ring - 1))

    @pl.when(bridge)
    def _():
        greet(position - 1 + 2 * core)

    load(*names[7:])
    entered = []

    def enter():
        if not entered:
            entered.append(1)
            pl.semaphore_wait(barrier, jnp.where(bridge, ring + 3, ring + 2))

    fine[...] = jnp.zeros_like(fine)
    halo_fine[...] = jnp.zeros_like(halo_fine)
    patches[...] = jnp.zeros_like(patches)

    def token_rows(s, m):
        return pl.ds(s * rows + m * window_tokens, window_tokens)

    def normalize(s):
        for m, gain in enumerate((gain_ct, gain_pet)):
            ready(("ct", "pet")[m], ("gain_ct", "gain_pet")[m])
            normed[token_rows(s, m), :] = rms_scale(tokens[m, s].astype(F32), gain[...].reshape(1, width))

    def project(s):
        both = pl.ds(s * rows, rows)
        if s == 0:
            for i, name in enumerate(("wq", "wk", "wv")):
                ready(name)
                cols = pl.ds(i * width, width)
                projected[both, cols] = matmul(normed[both, :], wqkv[:, cols]).astype(BF16)
        else:
            projected[both, :] = matmul(normed[both, :], wqkv[...]).astype(BF16)

    low_half = lax.broadcasted_iota(jnp.int32, (1, SUB), 1) < DH
    low = jnp.where(low_half, 1.0, 0.0).astype(BF16)
    high = jnp.where(low_half, 0.0, 1.0).astype(BF16)
    ones = jnp.concatenate(
        [jnp.broadcast_to(low, (window_tokens, SUB)), jnp.broadcast_to(high, (window_tokens, SUB))], axis=0
    )

    def attention(s):
        for m in range(2):
            own, other = token_rows(s, m), token_rows(s, 1 - m)
            for pair in range(width // SUB):
                cols = pl.ds(pair * SUB, SUB)
                key = projected[other, pl.ds(width + pair * SUB, SUB)]
                value = projected[other, pl.ds(2 * width + pair * SUB, SUB)]
                scores = lax.dot_general(
                    projected[own, cols], jnp.concatenate([key * low, key * high], axis=0),
                    (((1,), (1,)), ((), ())), preferred_element_type=F32,
                )
                probs = []
                for h in range(2):
                    part = scores[:, h * window_tokens : (h + 1) * window_tokens]
                    row_max = jnp.max(part, axis=-1, keepdims=True)
                    probs.append(jnp.exp2((part - row_max) * (math.log2(math.e) / DH**0.5)).astype(BF16))
                heads = matmul(
                    jnp.concatenate(probs, axis=1),
                    jnp.concatenate([jnp.concatenate([value * low, value * high], axis=0), ones], axis=1),
                )
                mixed[own, cols] = (heads[:, :SUB] / heads[:, SUB:]).astype(BF16)

    def forward(s):
        both = pl.ds(s * rows, rows)
        ready("wo", "gain_ffn")
        for m in range(2):
            own = token_rows(s, m)
            mid = tokens[m, s].astype(F32) + matmul(mixed[own, :], wo[...])
            middle[own, :] = mid
            normed[own, :] = rms_scale(mid, gain_ffn[...].reshape(1, width))
        ready("wup")
        block = 512 if inner % 512 == 0 else inner
        for start in range(0, inner, block):
            cols = pl.ds(start, block)
            inputs = matmul(normed[both, :], wup[:, cols])
            inside = inputs * (GELU_ONE + GELU_THREE * (inputs * inputs))
            active = inputs + inputs * jnp.tanh(inside)
            hidden[pl.ds(s * window_tokens, window_tokens), cols] = (
                0.5 * (active[:window_tokens] + active[window_tokens:])
            ).astype(BF16)

    def lower(s, c):
        ready("wdown")
        cols = pl.ds(c * cut, cut)
        total = (
            middle[token_rows(s, 0), cols] + middle[token_rows(s, 1), cols]
            + matmul(hidden[pl.ds(s * window_tokens, window_tokens), :], wdown[:, cols])
        )
        joined[s, c] = total.astype(BF16).reshape(WDEP, cells, cut)

    def remote(src, dst, send, recv, target):
        return pltpu.make_async_remote_copy(
            src_ref=src, dst_ref=dst, send_sem=send, recv_sem=recv,
            device_id={"brick": target}, device_id_type=MESH,
        )

    def near_pair(s, link, there, c):
        pick = (lambda ref, at: ref.at[s, at]) if c is None else (lambda ref, at: ref.at[s, at, c])
        c = 0 if c is None else c
        return remote(
            pick(share, link), pick(got, there), send_x.at[s, link, c], recv_x.at[s, there, c], near(link)
        )

    def near_copy(s, link, c=None):
        return near_pair(s, link, 1 if link == 1 else 2 + core, c)

    def near_arrival(s, link, c=None):
        return near_pair(s, link, link, c)

    def depth_of(anchor, at):
        return jnp.bitwise_and(at - anchor, WDEP - 1)

    def fetch(s, c, link, anchor):
        target = near(link) % 4 if link else partner % 4
        own = target + 1 - 2 * (target % 2) if link else target
        share[s, link, c] = joined[s, c, depth_of(anchor, own)]

    def source(s, link):
        slot = (near(link) if link else position) * slots + s
        anchor = anchor_ref[slot]
        depth = depth_of(anchor, kept)
        weight = count_ref[slot].astype(F32) * (1.0 / (2.0 * window_tokens)) * bell_at(depth)
        return (anchor + depth) // 4, weight

    def gather(s, c, z, sources):
        total = None
        for link, (where, weight) in enumerate(sources):
            block = (got if link else share)[s, link, c].astype(F32) * jnp.where(where == z, weight, 0.0)
            total = block if total is None else total + block
        return total

    def deep_pair(c, z, there):
        return remote(
            sum_z.at[c, z], got_z.at[c, there], send_z.at[c, z], recv_z.at[c, there], z * 4 + kept
        )

    last = slots - 1
    for s in range(slots):
        normalize(s)
    for s in range(slots):
        project(s)
        attention(s)
        forward(s)
        if s == 0:
            ready("anchor", "count")
            enter()
        anchor = anchor_ref[position * slots + s]
        if s < last:
            for c in range(pieces):
                lower(s, c)
            for link in (1, 2, 3):
                for c in range(pieces):
                    fetch(s, c, link, anchor)
                near_copy(s, link).start()
            for c in range(pieces):
                fetch(s, c, 0, anchor)
        else:
            for c in range(pieces):
                lower(s, c)
                for link in (1, 2, 3):
                    fetch(s, c, link, anchor)
                    near_copy(s, link, c).start()
                fetch(s, c, 0, anchor)
    for s in range(last):
        sources = [source(s, link) for link in range(4)]
        for link in range(1, 4):
            near_arrival(s, link).wait_recv()
        for c in range(pieces):
            for z in range(ring):
                block = gather(s, c, z, sources)
                early[c, z] = block if s == 0 else early[c, z] + block
    sources = [source(last, link) for link in range(4)]

    def send_deep(c, planes):
        for z in planes:
            total = gather(last, c, z, sources)
            if last:
                total = total + early[c, z]
            sum_z[c, z] = total.astype(BF16)
            deep_pair(c, z, deep).start()

    soon = ring // 2
    for c in range(pieces):
        for link in range(1, 4):
            near_arrival(last, link, c).wait_recv()
        send_deep(c, range(soon))
    for z in range(soon, ring):
        for c in range(pieces):
            send_deep(c, [z])
    ready("anchor_row", "count_row", "wupc", "wconv")
    row = (1, bricks * slots)
    denominator = jnp.sum(
        bell_at(position - anchor_row[...].reshape(row))
        * (count_row[...].reshape(row).astype(F32) * (1.0 / (2.0 * window_tokens))),
        axis=-1, keepdims=True,
    )
    inverse = 1.0 / jnp.maximum(denominator, 1.0)
    def edge_left():
        return remote(edge.at[0], got_edge.at[1], send_edge.at[0], recv_edge.at[1], position - 1)

    def edge_right():
        return remote(edge.at[1], got_edge.at[0], send_edge.at[1], recv_edge.at[0], position + 1)

    features = []
    for c in range(pieces):
        numerator = None
        for z in range(ring):
            deep_pair(c, z, z).wait_recv()
            block = got_z[c, z].astype(F32)
            numerator = block if numerator is None else numerator + block
        features.append((numerator * inverse).astype(BF16))

    for a, has_side, send in ((0, position > 0, edge_left), (1, position < bricks - 1, edge_right)):
        raised = None
        for c in range(pieces):
            part = matmul(features[c], wupc[pl.ds(c * cut, cut), pl.ds(a * 4 * channels, 4 * channels)])
            raised = part if raised is None else raised + part
        raised = raised.astype(BF16).astype(F32)
        for b in range(2):
            for c in range(2):
                at = (b * 2 + c) * channels
                for y in range(PY):
                    fine[a, 2 * y + b, pl.ds(8 + c, PX, stride=2), :] = raised[
                        y * PX : (y + 1) * PX, at : at + channels
                    ]
        edge[a] = jnp.maximum(fine[a, :, 8 : 8 + 2 * PX, :], 0.0).astype(BF16)

        @pl.when(has_side)
        def _():
            send().start()

    line = 2 * PX
    plane_rows = 2 * PY * line

    def fill(source, a, layer):
        for y in range(2 * PY):
            for dx in range(3):
                patches[layer, pl.ds((1 + y) * line, line), pl.ds(dx * channels, channels)] = jnp.maximum(
                    source[a, y, 7 + dx : 7 + dx + line, :], 0.0
                ).astype(BF16)

    def taps(layer, dz):
        acc = None
        for dy in range(3):
            term = matmul(
                patches[layer, pl.ds(dy * line, plane_rows), :],
                wconv[pl.ds((dz * 3 + dy) * 3 * channels, 3 * channels), :],
            )
            acc = term if acc is None else acc + term
        return acc

    fill(fine, 0, 1)
    fill(fine, 1, 2)
    upper = taps(1, 1) + taps(2, 2)
    lower_ = taps(1, 0) + taps(2, 1)

    for link in range(1, 4):
        for s in range(last):
            near_copy(s, link).wait_send()
        for c in range(pieces):
            near_copy(last, link, c).wait_send()
    for c in range(pieces):
        for z in range(ring):
            deep_pair(c, z, deep).wait_send()

    conv[0] = upper
    conv[1] = lower_

    def halo(end):
        @pl.when((position > 0) if end == 0 else (position < bricks - 1))
        def _():
            if end == 0:
                remote(edge.at[1], got_edge.at[0], send_edge.at[1], recv_edge.at[0], position - 1).wait_recv()
            else:
                remote(edge.at[0], got_edge.at[1], send_edge.at[0], recv_edge.at[1], position + 1).wait_recv()
            halo_fine[end, :, 8 : 8 + line, :] = got_edge[end].astype(F32)
            fill(halo_fine, end, 3 * end)
            conv[end] = conv[end] + taps(3 * end, 2 * end)

    @pl.when(core == 0)
    def _():
        halo(1)
        halo(0)

    @pl.when(core == 1)
    def _():
        halo(0)
        halo(1)

    @pl.when(position > 0)
    def _():
        edge_left().wait_send()

    @pl.when(position < bricks - 1)
    def _():
        edge_right().wait_send()

    for a in range(2):
        own = fine[a, :, 8 : 8 + line, :]
        out_ref[a] = (own + conv[a].reshape(own.shape)).astype(BF16)


def on_device(
    ct_win, pet_win, placed_anchor, placed_count, norm_ct, norm_pet, norm_ffn,
    w_query, w_key, w_value, w_out, w_up, w_down, w_upconv, w_conv,
):
    slots, window_tokens, width = ct_win.shape
    rows = 2 * slots * window_tokens
    bricks = lax.axis_size("brick")
    ring = bricks // 4
    cells = window_tokens // WDEP
    channels = w_conv.shape[1]
    line = 2 * PX
    cut = 256 if width % 256 == 0 else width
    pieces = width // cut
    dma = pltpu.SemaphoreType.DMA
    block = (cells, cut)

    def like(array):
        return pltpu.VMEM(array.shape, array.dtype)

    return pl.pallas_call(
        functools.partial(kernel, bricks),
        out_shape=pltpu.VMEM((2, 2 * PY, line, channels), BF16),
        in_specs=[pl.BlockSpec(memory_space=pl.ANY)] * 15,
        out_specs=pl.BlockSpec(memory_space=pltpu.VMEM),
        scratch_shapes=[
            pltpu.SMEM(placed_anchor.shape, jnp.int32), pltpu.SMEM(placed_count.shape, jnp.int32),
            like(placed_anchor), like(placed_count), like(norm_ct), like(norm_pet), like(norm_ffn),
            pltpu.VMEM((2,) + ct_win.shape, BF16),
            pltpu.VMEM((width, 3 * width), BF16), like(w_out), like(w_up), like(w_down),
            like(w_upconv), like(w_conv),
            pltpu.VMEM((rows, width), BF16),
            pltpu.VMEM((rows, 3 * width), BF16),
            pltpu.VMEM((rows, width), BF16),
            pltpu.VMEM((rows, width), F32),
            pltpu.VMEM((slots * window_tokens, w_up.shape[1]), BF16),
            pltpu.VMEM((slots, pieces, WDEP) + block, BF16),
            pltpu.VMEM((slots, 4, pieces) + block, BF16),
            pltpu.VMEM((slots, 4, pieces) + block, BF16),
            pltpu.VMEM((pieces, ring) + block, F32),
            pltpu.VMEM((pieces, ring) + block, BF16),
            pltpu.VMEM((pieces, ring) + block, BF16),
            pltpu.VMEM((2, 2 * PY, line + 16, channels), F32),
            pltpu.VMEM((2, 2 * PY, line + 16, channels), F32),
            pltpu.VMEM((2, 2 * PY, line, channels), BF16),
            pltpu.VMEM((2, 2 * PY, line, channels), BF16),
            pltpu.VMEM((4, (2 * PY + 2) * line, 3 * channels), BF16),
            pltpu.VMEM((2, 2 * PY * line, channels), F32),
            dma((17,)), dma((slots, 4, pieces)), dma((slots, 4, pieces)),
            dma((pieces, ring)), dma((pieces, ring)), dma((2,)), dma((2,)),
        ],
        compiler_params=pltpu.CompilerParams(
            collective_id=0, has_side_effects=True, vmem_limit_bytes=62 * 1024 * 1024
        ),
        name="windows",
    )(
        placed_anchor, placed_count, norm_ct, norm_pet, norm_ffn,
        ct_win, pet_win, w_query, w_key, w_value, w_out, w_up, w_down, w_upconv, w_conv,
    )


def solution(mesh):
    split = P(("groups", "brick"), None, None)
    return jax.shard_map(
        on_device,
        mesh=mesh,
        in_specs=(split, split, P("groups"), P("groups")) + (P(),) * 11,
        out_specs=P(("groups", "brick"), None, None, None),
        check_vma=False,
    )
```

```python
import functools
import math

import jax
import jax.numpy as jnp
from jax import lax
from jax.experimental import pallas as pl
from jax.experimental.pallas import tpu as pltpu
from jax.sharding import PartitionSpec as P

DH = 64
PY = 4
PX = 8
WDEP = 4
SUB = 128

epsilon = 1e-06
GELU_ONE = math.sqrt(2.0 / math.pi)
GELU_THREE = 0.044715 * GELU_ONE
F32 = jnp.float32
BF16 = jnp.bfloat16
MESH = pl.DeviceIdType.MESH


def rms_scale(inputs, gain_vec):
    mean_square = jnp.mean(inputs * inputs, axis=-1, keepdims=True)
    return (inputs * lax.rsqrt(mean_square + epsilon) * gain_vec).astype(BF16)


def matmul(left, right):
    return jnp.dot(left, right, preferred_element_type=F32)


def bell_at(depth):
    spread = WDEP / 4.0
    value = jnp.where(depth == depth, jnp.float32(0.0), jnp.float32(0.0))
    for i in range(WDEP):
        offset = i - (WDEP - 1) / 2.0
        value = jnp.where(depth == i, jnp.float32(math.exp(-offset * offset / (2.0 * spread * spread))), value)
    return value


def kernel(
    bricks,
    anchor_hbm, count_hbm, gain_ct_hbm, gain_pet_hbm, gain_ffn_hbm,
    ct_hbm, pet_hbm, wq_hbm, wk_hbm, wv_hbm, wo_hbm, wup_hbm, wdown_hbm, wupc_hbm, wconv_hbm,
    out_ref,
    anchor_ref, count_ref, anchor_row, count_row, gain_ct, gain_pet, gain_ffn,
    tokens, wqkv, wo, wup, wdown, wupc, wconv,
    normed, projected, mixed, middle, hidden, joined,
    share, got, early, sum_z, got_z,
    fine, halo_fine, edge, got_edge, patches, conv,
    load_sem, send_x, recv_x, send_z, recv_z, send_edge, recv_edge,
):
    position = lax.axis_index("brick")
    ring = bricks // 4
    place = position % 4
    core = position % 2
    side = (position // 2) % 2
    kept = place + 1 - 2 * core
    deep = position // 4

    slots, window_tokens, width = ct_hbm.shape
    rows = 2 * window_tokens
    cells = window_tokens // WDEP
    channels = wconv.shape[1]
    inner = wup.shape[1]
    pieces, cut = sum_z.shape[0], sum_z.shape[3]

    plan = {
        "ct": (ct_hbm, tokens.at[0]), "pet": (pet_hbm, tokens.at[1]),
        "gain_ct": (gain_ct_hbm, gain_ct), "gain_pet": (gain_pet_hbm, gain_pet),
        "wq": (wq_hbm, wqkv.at[:, pl.ds(0, width)]),
        "wk": (wk_hbm, wqkv.at[:, pl.ds(width, width)]),
        "wv": (wv_hbm, wqkv.at[:, pl.ds(2 * width, width)]),
        "gain_ffn": (gain_ffn_hbm, gain_ffn),
        "wo": (wo_hbm, wo), "wup": (wup_hbm, wup), "wdown": (wdown_hbm, wdown),
        "anchor": (anchor_hbm, anchor_ref), "count": (count_hbm, count_ref),
        "anchor_row": (anchor_hbm, anchor_row), "count_row": (count_hbm, count_row),
        "wupc": (wupc_hbm, wupc), "wconv": (wconv_hbm, wconv),
    }
    loads = {
        name: pltpu.make_async_copy(src, dst, load_sem.at[i]) for i, (name, (src, dst)) in enumerate(plan.items())
    }
    names = list(plan)
    waited = set()

    def load(*which):
        for name in which:
            loads[name].start()

    def ready(*which):
        for name in which:
            if name not in waited:
                waited.add(name)
                loads[name].wait()

    load(*names[:7])

    barrier = pltpu.get_barrier_semaphore()

    def greet(target):
        pl.semaphore_signal(barrier, inc=1, device_id={"brick": target}, device_id_type=MESH)

    partner = position + 1 - 2 * core
    across = position - place + 2 - 2 * side

    def near(link):
        return partner if link == 1 else across + link - 2

    for link in range(1, 4):
        greet(near(link))
    for step in range(1, ring):
        greet(lax.rem(deep + step, ring) * 4 + kept)
    bridge = ((place == 0) & (deep > 0)) | ((place == 3) & (deep < ring - 1))

    @pl.when(bridge)
    def _():
        greet(position - 1 + 2 * core)

    load(*names[7:])
    entered = []

    def enter():
        if not entered:
            entered.append(1)
            pl.semaphore_wait(barrier, jnp.where(bridge, ring + 3, ring + 2))

    fine[...] = jnp.zeros_like(fine)
    halo_fine[...] = jnp.zeros_like(halo_fine)
    patches[...] = jnp.zeros_like(patches)

    def token_rows(s, m):
        return pl.ds(s * rows + m * window_tokens, window_tokens)

    def normalize(s):
        for m, gain in enumerate((gain_ct, gain_pet)):
            ready(("ct", "pet")[m], ("gain_ct", "gain_pet")[m])
            normed[token_rows(s, m), :] = rms_scale(tokens[m, s].astype(F32), gain[...].reshape(1, width))

    def project(s):
        both = pl.ds(s * rows, rows)
        if s == 0:
            for i, name in enumerate(("wq", "wk", "wv")):
                ready(name)
                cols = pl.ds(i * width, width)
                projected[both, cols] = matmul(normed[both, :], wqkv[:, cols]).astype(BF16)
        else:
            projected[both, :] = matmul(normed[both, :], wqkv[...]).astype(BF16)

    low_half = lax.broadcasted_iota(jnp.int32, (1, SUB), 1) < DH
    low = jnp.where(low_half, 1.0, 0.0).astype(BF16)
    high = jnp.where(low_half, 0.0, 1.0).astype(BF16)
    ones = jnp.concatenate(
        [jnp.broadcast_to(low, (window_tokens, SUB)), jnp.broadcast_to(high, (window_tokens, SUB))], axis=0
    )

    def attention(s):
        for m in range(2):
            own, other = token_rows(s, m), token_rows(s, 1 - m)
            for pair in range(width // SUB):
                cols = pl.ds(pair * SUB, SUB)
                key = projected[other, pl.ds(width + pair * SUB, SUB)]
                value = projected[other, pl.ds(2 * width + pair * SUB, SUB)]
                scores = lax.dot_general(
                    projected[own, cols], jnp.concatenate([key * low, key * high], axis=0),
                    (((1,), (1,)), ((), ())), preferred_element_type=F32,
                )
                probs = []
                for h in range(2):
                    part = scores[:, h * window_tokens : (h + 1) * window_tokens]
                    row_max = jnp.max(part, axis=-1, keepdims=True)
                    probs.append(jnp.exp2((part - row_max) * (math.log2(math.e) / DH**0.5)).astype(BF16))
                heads = matmul(
                    jnp.concatenate(probs, axis=1),
                    jnp.concatenate([jnp.concatenate([value * low, value * high], axis=0), ones], axis=1),
                )
                mixed[own, cols] = (heads[:, :SUB] / heads[:, SUB:]).astype(BF16)

    def forward(s):
        both = pl.ds(s * rows, rows)
        ready("wo", "gain_ffn")
        for m in range(2):
            own = token_rows(s, m)
            mid = tokens[m, s].astype(F32) + matmul(mixed[own, :], wo[...])
            middle[own, :] = mid
            normed[own, :] = rms_scale(mid, gain_ffn[...].reshape(1, width))
        ready("wup")
        block = 512 if inner % 512 == 0 else inner
        for start in range(0, inner, block):
            cols = pl.ds(start, block)
            inputs = matmul(normed[both, :], wup[:, cols])
            inside = inputs * (GELU_ONE + GELU_THREE * (inputs * inputs))
            active = inputs + inputs * jnp.tanh(inside)
            hidden[pl.ds(s * window_tokens, window_tokens), cols] = (
                0.5 * (active[:window_tokens] + active[window_tokens:])
            ).astype(BF16)

    def lower(s, c):
        ready("wdown")
        cols = pl.ds(c * cut, cut)
        total = (
            middle[token_rows(s, 0), cols] + middle[token_rows(s, 1), cols]
            + matmul(hidden[pl.ds(s * window_tokens, window_tokens), :], wdown[:, cols])
        )
        joined[s, c] = total.astype(BF16).reshape(WDEP, cells, cut)

    def remote(src, dst, send, recv, target):
        return pltpu.make_async_remote_copy(
            src_ref=src, dst_ref=dst, send_sem=send, recv_sem=recv,
            device_id={"brick": target}, device_id_type=MESH,
        )

    def near_pair(s, link, there, c):
        pick = (lambda ref, at: ref.at[s, at]) if c is None else (lambda ref, at: ref.at[s, at, c])
        c = 0 if c is None else c
        return remote(
            pick(share, link), pick(got, there), send_x.at[s, link, c], recv_x.at[s, there, c], near(link)
        )

    def near_copy(s, link, c=None):
        return near_pair(s, link, 1 if link == 1 else 2 + core, c)

    def near_arrival(s, link, c=None):
        return near_pair(s, link, link, c)

    def depth_of(anchor, at):
        return jnp.bitwise_and(at - anchor, WDEP - 1)

    def fetch(s, c, link, anchor):
        target = near(link) % 4 if link else partner % 4
        own = target + 1 - 2 * (target % 2) if link else target
        share[s, link, c] = joined[s, c, depth_of(anchor, own)]

    def source(s, link):
        slot = (near(link) if link else position) * slots + s
        anchor = anchor_ref[slot]
        depth = depth_of(anchor, kept)
        weight = count_ref[slot].astype(F32) * (1.0 / (2.0 * window_tokens)) * bell_at(depth)
        return (anchor + depth) // 4, weight

    def gather(s, c, z, sources):
        total = None
        for link, (where, weight) in enumerate(sources):
            block = (got if link else share)[s, link, c].astype(F32) * jnp.where(where == z, weight, 0.0)
            total = block if total is None else total + block
        return total

    def deep_pair(c, z, there):
        return remote(
            sum_z.at[c, z], got_z.at[c, there], send_z.at[c, z], recv_z.at[c, there], z * 4 + kept
        )

    last = slots - 1
    for s in range(slots):
        normalize(s)
    for s in range(slots):
        project(s)
        attention(s)
        forward(s)
        if s == 0:
            ready("anchor", "count")
            enter()
        anchor = anchor_ref[position * slots + s]
        if s < last:
            for c in range(pieces):
                lower(s, c)
            for link in (1, 2, 3):
                for c in range(pieces):
                    fetch(s, c, link, anchor)
                near_copy(s, link).start()
            for c in range(pieces):
                fetch(s, c, 0, anchor)
        else:
            for c in range(pieces):
                lower(s, c)
                for link in (1, 2, 3):
                    fetch(s, c, link, anchor)
                    near_copy(s, link, c).start()
                fetch(s, c, 0, anchor)
    for s in range(last):
        sources = [source(s, link) for link in range(4)]
        for link in range(1, 4):
            near_arrival(s, link).wait_recv()
        for c in range(pieces):
            for z in range(ring):
                block = gather(s, c, z, sources)
                early[c, z] = block if s == 0 else early[c, z] + block
    sources = [source(last, link) for link in range(4)]

    def send_deep(c, planes):
        for z in planes:
            total = gather(last, c, z, sources)
            if last:
                total = total + early[c, z]
            sum_z[c, z] = total.astype(BF16)
            deep_pair(c, z, deep).start()

    soon = 1
    for c in range(pieces):
        for link in range(1, 4):
            near_arrival(last, link, c).wait_recv()
        send_deep(c, range(soon))
    for z in range(soon, ring):
        for c in range(pieces):
            send_deep(c, [z])
    ready("anchor_row", "count_row", "wupc", "wconv")
    row = (1, bricks * slots)
    denominator = jnp.sum(
        bell_at(position - anchor_row[...].reshape(row))
        * (count_row[...].reshape(row).astype(F32) * (1.0 / (2.0 * window_tokens))),
        axis=-1, keepdims=True,
    )
    inverse = 1.0 / jnp.maximum(denominator, 1.0)
    def edge_left():
        return remote(edge.at[0], got_edge.at[1], send_edge.at[0], recv_edge.at[1], position - 1)

    def edge_right():
        return remote(edge.at[1], got_edge.at[0], send_edge.at[1], recv_edge.at[0], position + 1)

    features = []
    for c in range(pieces):
        numerator = None
        for z in range(ring):
            deep_pair(c, z, z).wait_recv()
            block = got_z[c, z].astype(F32)
            numerator = block if numerator is None else numerator + block
        features.append((numerator * inverse).astype(BF16))

    for a, has_side, send in ((0, position > 0, edge_left), (1, position < bricks - 1, edge_right)):
        raised = None
        for c in range(pieces):
            part = matmul(features[c], wupc[pl.ds(c * cut, cut), pl.ds(a * 4 * channels, 4 * channels)])
            raised = part if raised is None else raised + part
        raised = raised.astype(BF16).astype(F32)
        for b in range(2):
            for c in range(2):
                at = (b * 2 + c) * channels
                for y in range(PY):
                    fine[a, 2 * y + b, pl.ds(8 + c, PX, stride=2), :] = raised[
                        y * PX : (y + 1) * PX, at : at + channels
                    ]
        edge[a] = jnp.maximum(fine[a, :, 8 : 8 + 2 * PX, :], 0.0).astype(BF16)

        @pl.when(has_side)
        def _():
            send().start()

    line = 2 * PX
    plane_rows = 2 * PY * line

    def fill(source, a, layer):
        for y in range(2 * PY):
            for dx in range(3):
                patches[layer, pl.ds((1 + y) * line, line), pl.ds(dx * channels, channels)] = jnp.maximum(
                    source[a, y, 7 + dx : 7 + dx + line, :], 0.0
                ).astype(BF16)

    def taps(layer, dz):
        acc = None
        for dy in range(3):
            term = matmul(
                patches[layer, pl.ds(dy * line, plane_rows), :],
                wconv[pl.ds((dz * 3 + dy) * 3 * channels, 3 * channels), :],
            )
            acc = term if acc is None else acc + term
        return acc

    fill(fine, 0, 1)
    fill(fine, 1, 2)
    upper = taps(1, 1) + taps(2, 2)
    lower_ = taps(1, 0) + taps(2, 1)

    for link in range(1, 4):
        for s in range(last):
            near_copy(s, link).wait_send()
        for c in range(pieces):
            near_copy(last, link, c).wait_send()
    for c in range(pieces):
        for z in range(ring):
            deep_pair(c, z, deep).wait_send()

    conv[0] = upper
    conv[1] = lower_

    def halo(end):
        @pl.when((position > 0) if end == 0 else (position < bricks - 1))
        def _():
            if end == 0:
                remote(edge.at[1], got_edge.at[0], send_edge.at[1], recv_edge.at[0], position - 1).wait_recv()
            else:
                remote(edge.at[0], got_edge.at[1], send_edge.at[0], recv_edge.at[1], position + 1).wait_recv()
            halo_fine[end, :, 8 : 8 + line, :] = got_edge[end].astype(F32)
            fill(halo_fine, end, 3 * end)
            conv[end] = conv[end] + taps(3 * end, 2 * end)

    @pl.when(core == 0)
    def _():
        halo(1)
        halo(0)

    @pl.when(core == 1)
    def _():
        halo(0)
        halo(1)

    @pl.when(position > 0)
    def _():
        edge_left().wait_send()

    @pl.when(position < bricks - 1)
    def _():
        edge_right().wait_send()

    for a in range(2):
        own = fine[a, :, 8 : 8 + line, :]
        out_ref[a] = (own + conv[a].reshape(own.shape)).astype(BF16)


def on_device(
    ct_win, pet_win, placed_anchor, placed_count, norm_ct, norm_pet, norm_ffn,
    w_query, w_key, w_value, w_out, w_up, w_down, w_upconv, w_conv,
):
    slots, window_tokens, width = ct_win.shape
    rows = 2 * slots * window_tokens
    bricks = lax.axis_size("brick")
    ring = bricks // 4
    cells = window_tokens // WDEP
    channels = w_conv.shape[1]
    line = 2 * PX
    cut = 256 if width % 256 == 0 else width
    pieces = width // cut
    dma = pltpu.SemaphoreType.DMA
    block = (cells, cut)

    def like(array):
        return pltpu.VMEM(array.shape, array.dtype)

    return pl.pallas_call(
        functools.partial(kernel, bricks),
        out_shape=pltpu.VMEM((2, 2 * PY, line, channels), BF16),
        in_specs=[pl.BlockSpec(memory_space=pl.ANY)] * 15,
        out_specs=pl.BlockSpec(memory_space=pltpu.VMEM),
        scratch_shapes=[
            pltpu.SMEM(placed_anchor.shape, jnp.int32), pltpu.SMEM(placed_count.shape, jnp.int32),
            like(placed_anchor), like(placed_count), like(norm_ct), like(norm_pet), like(norm_ffn),
            pltpu.VMEM((2,) + ct_win.shape, BF16),
            pltpu.VMEM((width, 3 * width), BF16), like(w_out), like(w_up), like(w_down),
            like(w_upconv), like(w_conv),
            pltpu.VMEM((rows, width), BF16),
            pltpu.VMEM((rows, 3 * width), BF16),
            pltpu.VMEM((rows, width), BF16),
            pltpu.VMEM((rows, width), F32),
            pltpu.VMEM((slots * window_tokens, w_up.shape[1]), BF16),
            pltpu.VMEM((slots, pieces, WDEP) + block, BF16),
            pltpu.VMEM((slots, 4, pieces) + block, BF16),
            pltpu.VMEM((slots, 4, pieces) + block, BF16),
            pltpu.VMEM((pieces, ring) + block, F32),
            pltpu.VMEM((pieces, ring) + block, BF16),
            pltpu.VMEM((pieces, ring) + block, BF16),
            pltpu.VMEM((2, 2 * PY, line + 16, channels), F32),
            pltpu.VMEM((2, 2 * PY, line + 16, channels), F32),
            pltpu.VMEM((2, 2 * PY, line, channels), BF16),
            pltpu.VMEM((2, 2 * PY, line, channels), BF16),
            pltpu.VMEM((4, (2 * PY + 2) * line, 3 * channels), BF16),
            pltpu.VMEM((2, 2 * PY * line, channels), F32),
            dma((17,)), dma((slots, 4, pieces)), dma((slots, 4, pieces)),
            dma((pieces, ring)), dma((pieces, ring)), dma((2,)), dma((2,)),
        ],
        compiler_params=pltpu.CompilerParams(
            collective_id=0, has_side_effects=True, vmem_limit_bytes=62 * 1024 * 1024
        ),
        name="windows",
    )(
        placed_anchor, placed_count, norm_ct, norm_pet, norm_ffn,
        ct_win, pet_win, w_query, w_key, w_value, w_out, w_up, w_down, w_upconv, w_conv,
    )


def solution(mesh):
    split = P(("groups", "brick"), None, None)
    return jax.shard_map(
        on_device,
        mesh=mesh,
        in_specs=(split, split, P("groups"), P("groups")) + (P(),) * 11,
        out_specs=P(("groups", "brick"), None, None, None),
        check_vma=False,
    )
```
